256 devices in a mesh: box: 64 (over x, z, core), col: 4 (over y).
Axes of the slice: x: 4, y: 4, z: 8, core: 2. Of those that a mesh axis runs over, the one named last changes fastest.
Arguments:
- child_maps: float32 [64, 1536, 1536], P('box', None, 'col'), may hold values from -13 to 14, as said below
- iface_one: int32 [64, 512], P('box'), may hold values from 0 to 1535, as said below
- iface_two: int32 [32, 512], replicated, may hold values from 0 to 3071, as said below
Outputs:
- parent_two: float32 [64, 6144, 1536], P('box', None, 'col')
The draws below stay inside these ranges and needn't reach their ends.
Inputs may be any that keep to these rules, and one draw needn't show every extreme that they name: `child_maps`: every child map is symmetric and positive definite. `iface_one`: row c lists 512 distinct points of child c; rows 2k and 2k+1 list the same physical points in the same order. `iface_two`: row p lists 512 distinct points of the first-level parent of children 2p and 2p+1 (points of child 2p+1 counted from 1536), none of them listed in iface_one for those children: first 256 points of child 2p, then 256 of child 2p+1. Rows 2j and 2j+1 list the same physical points in the same order.
All inputs are finite; a program needn't handle non-finite values.
Results may differ from the reference program's by a relative error of at most 0.00005.
Values sent between devices are 32-bit elements; how exact they have to be, the bound alone decides.
No kernel may reach another device: no remote copies, remote signals or barrier semaphores. Data moves between devices by JAX's collectives and lax.ppermute only.
A program may use at most 128 MiB of HBM per device.

```python
import jax
import jax.numpy as jnp
from jax import lax

M = 1536
IFACE = 512
CHILDREN = 64


def shuffled(child_key):
    return jax.random.permutation(child_key, M)


def interface_lists(base_key):
    child_keys = jax.random.split(jax.random.fold_in(base_key, 7), CHILDREN)
    orders = jax.vmap(shuffled)(child_keys)
    first_lists = orders[:, :IFACE]
    chosen = orders[:, IFACE:IFACE + IFACE // 2]
    offset = jnp.arange(CHILDREN, dtype=jnp.int32) % 2 * M
    chosen = chosen + offset[:, None]
    second_lists = chosen.reshape(CHILDREN // 2, IFACE)
    return (first_lists.astype(jnp.int32), second_lists.astype(jnp.int32))


def draw_iface_one(key, part):
    return interface_lists(key)[0]


def draw_iface_two(key, part):
    return interface_lists(key)[1]


def draw_child_maps(key, part):
    weight_key, diagonal_key = jax.random.split(jax.random.fold_in(key, 3), 2)
    half_width = M // 2
    factor = jax.random.uniform(weight_key, (CHILDREN, M, half_width), jnp.float32, -1.7320508, 1.7320508)
    diagonal = jax.random.uniform(diagonal_key, (CHILDREN, M), jnp.float32, 0.5, 2.0)
    gram_part = jnp.einsum('cmh,cnh->cmn', factor, factor) / half_width
    gram_part = 0.5 * (gram_part + jnp.swapaxes(gram_part, 1, 2))
    return gram_part + diagonal[:, :, None] * jnp.eye(M, dtype=jnp.float32)[None, :, :]


def setup_inputs(seed: int = 0) -> dict:
    streams_of = jax.random.split(jax.random.key(seed), 4)
    return {
        "child_maps": draw_child_maps(jax.random.fold_in(streams_of[3], 71), 0),
        "iface_one": draw_iface_one(jax.random.fold_in(streams_of[3], 71), 0),
        "iface_two": draw_iface_two(jax.random.fold_in(streams_of[3], 71), 0),
    }


def block_pair(first_half, second):
    count_all = first_half.shape[0]
    blank_rows = jnp.zeros((count_all, count_all), jnp.float32)
    upper_rows = jnp.concatenate([first_half, blank_rows], axis=1)
    lower_rows = jnp.concatenate([blank_rows, second], axis=1)
    return jnp.concatenate([upper_rows, lower_rows], axis=0)

def eliminate(joined, first_points, second_points):
    edge_rows = joined[first_points, :] + joined[second_points, :]
    edge_cols = joined[:, first_points] + joined[:, second_points]
    schur_matrix = edge_rows[:, first_points] + edge_rows[:, second_points]
    solved = jnp.linalg.solve(schur_matrix, edge_rows)
    count_all = joined.shape[0]
    matches = jnp.zeros((count_all,), jnp.float32).at[first_points].add(1.0).at[second_points].add(1.0)
    remain = 1.0 - matches
    reduced = joined - jnp.dot(edge_cols.astype(jnp.float32), solved.astype(jnp.float32), precision=lax.Precision.HIGHEST, preferred_element_type=jnp.float32)
    return reduced * remain[:, None] * remain[None, :]

def merge_one(member):
    map_pair, points = member
    return eliminate(block_pair(map_pair[0], map_pair[1]), points[0], points[1] + M)

def merge_two(member):
    map_pair, points = member
    whole_map = eliminate(block_pair(map_pair[0], map_pair[1]), points[0], points[1] + 2 * M)
    return whole_map.reshape(4 * M, 4, M).transpose(1, 0, 2)

def reference(child_maps, iface_one, iface_two):
    map_pairs = child_maps.reshape(CHILDREN // 2, 2, M, M)
    list_pairs = iface_one.reshape(CHILDREN // 2, 2, IFACE)
    parents = lax.map(merge_one, (map_pairs, list_pairs))
    quad_maps = parents.reshape(CHILDREN // 4, 2, 2 * M, 2 * M)
    list_quads = iface_two.reshape(CHILDREN // 4, 2, IFACE)
    result = lax.map(merge_two, (quad_maps, list_quads))
    return result.reshape(CHILDREN, 4 * M, M)
```

```python
import functools

import jax
import jax.numpy as jnp
from jax import lax
from jax.experimental import pallas as pl
from jax.experimental.pallas import tpu as pltpu
from jax.sharding import PartitionSpec as P

F32 = jnp.float32
BF16 = jnp.bfloat16
HI = lax.Precision.HIGHEST
COLS = 4
IFACE = 512
HALF = 256
EDGE = IFACE + HALF


VMEM = pl.BlockSpec(memory_space=pltpu.VMEM)
SMEM = pl.BlockSpec(memory_space=pltpu.SMEM)
ANY = pl.BlockSpec(memory_space=pl.ANY)


def call(body, name, outs, n_smem, n_in, flops, nbytes, scratch=()):
    return pl.pallas_call(
        body,
        name=name,
        out_shape=outs,
        in_specs=[SMEM] * n_smem + [VMEM] * n_in,
        out_specs=jax.tree.map(lambda _: VMEM, outs),
        scratch_shapes=scratch,
        cost_estimate=pl.CostEstimate(flops=flops, bytes_accessed=nbytes, transcendentals=0),
        compiler_params=pltpu.CompilerParams(vmem_limit_bytes=56 * 2**20),
    )


def shape(*dims):
    return jax.ShapeDtypeStruct(dims, F32)


def lane_of(v, j):
    return jnp.broadcast_to(v[:, j : j + 1], v.shape)


def row_of(v, r):
    return jnp.broadcast_to(v[r : r + 1, :], v.shape)


def eliminate_eight(rows, p, lane, sub):
    off = 8 * p
    top = rows[p]
    cols = [lane_of(top, off + j) for j in range(8)]
    rest = {i: [lane_of(rows[i], off + j) for j in range(8)] for i in range(16) if i != p}
    for r in range(8):
        inv = 1.0 / row_of(cols[r], r)
        mult = jnp.where(sub == r, -1.0, cols[r])
        scaled = jnp.where(lane == off + r, inv, row_of(top, r) * inv)
        top = jnp.where((sub == r) | (lane == off + r), 0.0, top) - mult * scaled
        for j in range(r + 1, 8):
            cols[j] = jnp.where(sub == r, 0.0, cols[j]) - mult * (row_of(cols[j], r) * inv)
    head = [row_of(top, j) for j in range(8)]
    inside = (lane >= off) & (lane < off + 8)
    out = list(rows)
    out[p] = top
    for i, c in rest.items():
        t = [c[j] * head[j] for j in range(8)]
        s = ((t[0] + t[1]) + (t[2] + t[3])) + ((t[4] + t[5]) + (t[6] + t[7]))
        out[i] = jnp.where(inside, 0.0, rows[i]) - s
    return out


def inverse_128(a):
    lane = lax.broadcasted_iota(jnp.int32, (8, 128), 1)
    sub = lax.broadcasted_iota(jnp.int32, (8, 128), 0)
    rows = [a[8 * i : 8 * i + 8, :] for i in range(16)]
    for p in range(16):
        rows = eliminate_eight(rows, p, lane, sub)
    return jnp.concatenate(rows, axis=0)


def dot(a, b):
    return jnp.dot(a, b, precision=HI, preferred_element_type=F32)


def dot_nt(a, b):
    return lax.dot_general(
        a, b, (((1,), (1,)), ((), ())), precision=HI, preferred_element_type=F32
    )


def dot_tn(a, b):
    return lax.dot_general(
        a, b, (((0,), (0,)), ((), ())), precision=HI, preferred_element_type=F32
    )


def inverse_in_place(ref):
    n, b = ref.shape[0], 128
    block_of_row = lax.broadcasted_iota(jnp.int32, (n, 1), 0) // b

    def step(i, _):
        o = pl.multiple_of(i * b, b)
        pivot = inverse_128(ref[pl.ds(o, b), pl.ds(o, b)])
        across = dot(pivot, ref[pl.ds(o, b), :])
        down = jnp.where(block_of_row == i, 0.0, ref[:, pl.ds(o, b)])
        rest = ref[...] - dot(down, across)
        left = -dot(down, pivot)
        ref[...] = rest
        ref[pl.ds(o, b), :] = across
        ref[:, pl.ds(o, b)] = left
        ref[pl.ds(o, b), pl.ds(o, b)] = pivot
        return 0

    lax.fori_loop(0, n // b, step, 0)


def inverse_kernel(a_ref, b_ref, o_ref):
    o_ref[...] = a_ref[...] + b_ref[...]
    inverse_in_place(o_ref)


def inverse_of_sum(a, b):
    n = a.shape[0]
    return call(inverse_kernel, "inverse", shape(n, n), 0, 2, 20 * n**3, 12 * n * n)(a, b)


def pick_rows(idx_ref, start, src, dst, dst_start, count, lanes):
    def eight(g, _):
        base = g * 8
        got = [src[pl.ds(idx_ref[start + base + i], 1), lanes] for i in range(8)]
        dst[pl.ds(pl.multiple_of(dst_start + base, 8), 8), :] = jnp.concatenate(got, axis=0)
        return 0

    lax.fori_loop(0, count // 8, eight, 0)


def gather_kernel(idx_ref, a_ref, pi_ref, pj_ref, rows):
    pick_rows(idx_ref, 0, a_ref, rows, 0, EDGE, slice(None))
    for k in range(0, IFACE, 128):
        pi_ref[:, k : k + 128] = rows[k : k + 128, :].T
    for k in range(0, HALF, 128):
        pj_ref[:, k : k + 128] = rows[IFACE + k : IFACE + k + 128, :].T


def stack_into(stack, own, right, left, far_a, far_b):
    w = own.shape[0]
    stack[0:w, :] = own[...]
    stack[w : 2 * w, :] = right[...]
    stack[2 * w : 2 * w + w // 2, :] = far_a[...]
    stack[2 * w + w // 2 : 3 * w, :] = far_b[...]
    stack[3 * w : 4 * w, :] = left[...]


def select_kernel(start, count, idx_ref, own, right, left, far_a, far_b, o_ref, stack):
    stack_into(stack, own, right, left, far_a, far_b)
    pick_rows(idx_ref, start, stack, o_ref, 0, count, slice(None))


def column_of(row, n):
    return jnp.broadcast_to(row, (128, n)).T


def middle_kernel(where, inv, xy_own, xy_sib, pi, pj, keep, m_ref, s_ref, gt_ref, x_all):
    parity = where[0]
    mine = pl.ds(pl.multiple_of(parity * HALF, HALF), HALF)
    other = pl.ds(pl.multiple_of((1 - parity) * HALF, HALF), HALF)
    x_all[:, mine] = xy_own[0:IFACE, :]
    x_all[:, other] = xy_sib[0:IFACE, :]
    m = dot(inv[...], x_all[...])
    m_ref[...] = m
    s_ref[...] = -dot_tn(xy_own[0:IFACE, :], m)
    s_ref[:, mine] = s_ref[:, mine] + xy_own[IFACE:EDGE, :]
    mask = jnp.tile(column_of(keep[...], pi.shape[0]), (1, IFACE // 128))
    gt_ref[...] = -dot(pi[...], m)
    gt_ref[:, mine] = gt_ref[:, mine] + pj[...]
    gt_ref[...] = gt_ref[...] * mask


def first_kernel(inv, pi, keep, w_ref):
    mask = jnp.tile(column_of(keep[...], pi.shape[0]), (1, IFACE // 128))
    w_ref[...] = dot(pi[...], inv[...]) * mask


def split(v):
    high = v.astype(BF16)
    return high, (v - high.astype(F32)).astype(BF16)


def three(a, b):
    def one(x, y):
        return jnp.dot(x, y, preferred_element_type=F32)

    return one(a[0], b[0]) + (one(a[0], b[1]) + one(a[1], b[0]))


def last_kernel(where, inv, m_ref, gt, w1t, a_ref, keep2, keep_col, *refs):
    n_in = 30
    ins, out = refs[:n_in], refs[n_in]
    edges, others, uv_hi, uv_lo, v_hi, v_lo, block, in_sems, out_sems = refs[n_in + 1 :]
    parity, quad, col = where[0], where[1], where[2]
    w = gt.shape[0]
    copies = []

    def load(src, dst):
        c = pltpu.make_async_copy(src, dst, in_sems.at[len(copies)])
        c.start()
        copies.append(c)

    places = [(0, 0, w), (1, 0, w), (3, 0, w), (2, 0, w // 2), (2, w // 2, w // 2)]
    for m in range(2):
        for k, (r, lo, size) in enumerate(places):
            load(ins[10 * m + k], edges.at[4 * m + r, pl.ds(lo, size), pl.ds(0, IFACE)])
            load(ins[10 * m + 5 + k], edges.at[4 * m + r, pl.ds(lo, size), pl.ds(IFACE, HALF)])
    for m in range(2):
        for k, (r, lo, size) in enumerate(places):
            load(ins[20 + 5 * m + k], others.at[4 * m + r, pl.ds(lo, size), :])

    vt = dot(gt[...], inv[...])
    ut = w1t[...] - dot_nt(vt, m_ref[...])
    u, v = split(ut.T), split(vt.T)
    for m in range(2):
        uv_hi[m, 0:IFACE, :], uv_lo[m, 0:IFACE, :] = u
    v_hi[...], v_lo[...] = v
    mine = pl.ds(pl.multiple_of(parity * HALF, HALF), HALF)
    other = pl.ds(pl.multiple_of((1 - parity) * HALF, HALF), HALF)
    for m, half in enumerate((mine, other)):
        uv_hi[m, IFACE:EDGE, :] = v_hi[half, :]
        uv_lo[m, IFACE:EDGE, :] = v_lo[half, :]
    for c in copies:
        c.wait()

    def place(m, r):
        o = (quad ^ m) * (COLS * w) + ((col + r) % COLS) * w
        return pl.ds(pl.multiple_of(o, w), w)

    def store(slot, m, r):
        return pltpu.make_async_copy(block.at[slot], out.at[place(m, r), :], out_sems.at[slot])

    for i in range(16):
        m, r, slot = i // 4, i % 4, i % 2
        if i >= 2:
            store(slot, (i - 2) // 4, (i - 2) % 4).wait()
        if m < 2:
            total = -three(split(edges[i]), (uv_hi[m], uv_lo[m]))
            rows = pl.ds(pl.multiple_of(((col + r) % COLS) * w, w), w)
            if m == 0:
                total = total + a_ref[rows, :] * keep_col[...]
            mask = column_of(keep2[m : m + 1, rows], w)
            block[slot] = total * jnp.tile(mask, (1, w // 128))
        else:
            block[slot] = -three(split(others[i - 8]), (v_hi[...], v_lo[...]))
        store(slot, m, r).start()
    for i in (14, 15):
        store(i % 2, i // 4, i % 4).wait()


def swapped(shard, apart):
    n = lax.axis_size("box")
    return lax.ppermute(shard, "box", [(i, i ^ apart) for i in range(n)])


def shifted(shard, by):
    return lax.ppermute(shard, "col", [((i + by) % COLS, i) for i in range(COLS)])


def after(value, *others):
    return lax.optimization_barrier((value, *others))[0]


def around(own):
    h = own.shape[0] // 2
    right, left = shifted(own, 1), shifted(own, -1)
    return own, right, left, shifted(right[:h], 1), shifted(left[h:], -1)


def local(child_maps, iface_one, iface_two):
    a = child_maps[0]
    boundary, w = a.shape
    box, col = lax.axis_index("box"), lax.axis_index("col")
    parity = box % 2
    own_one = iface_one[0]
    group = lax.dynamic_index_in_dim(iface_two, box // 2, 0, keepdims=False)
    own_two = lax.dynamic_slice_in_dim(group, parity * HALF, HALF) - parity * boundary
    points = jnp.concatenate([own_one, own_two])
    where = jnp.stack([parity, box % 4, col]).astype(jnp.int32)

    pi, pj = call(
        gather_kernel, "gather", (shape(w, IFACE), shape(w, HALF)), 1, 1, 0, 4 * boundary * w,
        [pltpu.VMEM((EDGE, w), F32)],
    )(points, a)
    pi_all = around(pi)
    pj_all = around(after(pj, *pi_all[3:]))

    matches = jnp.arange(boundary, dtype=jnp.int32)[None, :] == points[:, None]
    keep = 1.0 - jnp.sum(matches.astype(F32), axis=0)
    keep_col = lax.dynamic_slice_in_dim(keep, col * w, w)[None, :]
    keep2 = jnp.stack([keep, swapped(keep, 1)])

    relative = (points - col * w) % boundary
    t_one = call(
        functools.partial(select_kernel, 0, IFACE), "select_one", shape(IFACE, IFACE), 1, 5,
        0, 8 * boundary * IFACE, [pltpu.VMEM((boundary, IFACE), F32)],
    )(relative, *pi_all)
    inv_one = inverse_of_sum(t_one, swapped(t_one, 1))

    xy = call(
        functools.partial(select_kernel, 0, EDGE), "select_two", shape(EDGE, HALF), 1, 5,
        0, 8 * boundary * HALF, [pltpu.VMEM((boundary, HALF), F32)],
    )(relative, *pj_all)
    xy_sib = swapped(xy, 1)
    m, s_half, gt = call(
        middle_kernel, "middle", (shape(IFACE, IFACE), shape(HALF, IFACE), shape(w, IFACE)), 1, 6,
        2**31, 2**22, [pltpu.VMEM((IFACE, IFACE), F32)],
    )(where, inv_one, xy, xy_sib, pi, pj, keep_col)
    s_half = s_half + swapped(s_half, 2)
    s_other = swapped(s_half, 1)
    first = jnp.where(parity == 0, s_half, s_other)
    second = jnp.where(parity == 0, s_other, s_half)
    schur_two = jnp.concatenate([first, second], axis=0)
    w1t = call(first_kernel, "first", shape(w, IFACE), 0, 3, 2**30, 2**22)(inv_one, pi, keep_col)
    gz_all = around(swapped(after(gt, s_half), 2))
    inv_two = inverse_of_sum(schur_two, jnp.zeros_like(schur_two))

    pi_sib = [swapped(v, 1) for v in pi_all]
    pj_sib = [swapped(v, 1) for v in pj_all]
    gz_sib = [swapped(v, 1) for v in gz_all]
    out = pl.pallas_call(
        last_kernel,
        name="last",
        out_shape=shape(COLS * boundary, w),
        in_specs=[SMEM] + [VMEM] * 7 + [ANY] * 30,
        out_specs=ANY,
        scratch_shapes=[
            pltpu.VMEM((8, w, EDGE), F32),
            pltpu.VMEM((8, w, IFACE), F32),
            pltpu.VMEM((2, EDGE, w), BF16),
            pltpu.VMEM((2, EDGE, w), BF16),
            pltpu.VMEM((IFACE, w), BF16),
            pltpu.VMEM((IFACE, w), BF16),
            pltpu.VMEM((2, w, w), F32),
            pltpu.SemaphoreType.DMA((30,)),
            pltpu.SemaphoreType.DMA((2,)),
        ],
        cost_estimate=pl.CostEstimate(flops=10**10, bytes_accessed=3 * 10**7, transcendentals=0),
        compiler_params=pltpu.CompilerParams(vmem_limit_bytes=56 * 2**20),
    )(
        where, inv_two, m, gt, w1t, a, keep2, keep_col,
        *pi_all, *pj_all, *pi_sib, *pj_sib, *gz_all, *gz_sib,
    )
    return out[None]


def solution(mesh):
    return jax.shard_map(
        local,
        mesh=mesh,
        in_specs=(P("box", None, "col"), P("box", None), P()),
        out_specs=P("box", None, "col"),
        check_vma=False,
    )
```

```python
import functools

import jax
import jax.numpy as jnp
from jax import lax
from jax.experimental import pallas as pl
from jax.experimental.pallas import tpu as pltpu
from jax.sharding import PartitionSpec as P

F32 = jnp.float32
BF16 = jnp.bfloat16
HI = lax.Precision.HIGHEST
COLS = 4
IFACE = 512
HALF = 256
EDGE = IFACE + HALF
PARTS = EDGE // HALF


PER = 8

VMEM = pl.BlockSpec(memory_space=pltpu.VMEM)
SMEM = pl.BlockSpec(memory_space=pltpu.SMEM)
ANY = pl.BlockSpec(memory_space=pl.ANY)


def call(body, outs, n_smem, n_in, flops, nbytes, scratch=()):
    return pl.pallas_call(
        body,
        out_shape=outs,
        in_specs=[SMEM] * n_smem + [VMEM] * n_in,
        out_specs=jax.tree.map(lambda _: VMEM, outs),
        scratch_shapes=scratch,
        cost_estimate=pl.CostEstimate(flops=flops, bytes_accessed=nbytes, transcendentals=0),
        compiler_params=pltpu.CompilerParams(vmem_limit_bytes=56 * 2**20),
    )


def shape(*dims):
    return jax.ShapeDtypeStruct(dims, F32)


def lane_of(v, j):
    return jnp.broadcast_to(v[:, j : j + 1], v.shape)


def row_of(v, r):
    return jnp.broadcast_to(v[r : r + 1, :], v.shape)


def eliminate_eight(rows, p, lane, sub):
    off = 8 * p
    full = [row_of(rows[p], k) for k in range(8)]
    e = {(k, j): lane_of(full[k], off + j) for k in range(8) for j in range(k, 8)}
    rest = {i: [lane_of(rows[i], off + j) for j in range(8)] for i in range(16) if i != p}
    inside = (lane >= off) & (lane < off + 8)
    full = [jnp.where(inside, jnp.where(lane == off + k, 1.0, 0.0), full[k]) for k in range(8)]
    low, inv = {}, []
    for k in range(8):
        inv.append(1.0 / e[k, k])
        for r in range(k + 1, 8):
            low[r, k] = e[k, r] * inv[k]
            full[r] = full[r] - low[r, k] * full[k]
        for r in range(k + 1, 8):
            for j in range(r, 8):
                e[r, j] = e[r, j] - low[r, k] * e[k, j]
    full = [full[k] * inv[k] for k in range(8)]
    for k in range(7, 0, -1):
        for r in range(k):
            full[r] = full[r] - low[k, r] * full[k]
    top = full[0]
    for k in range(1, 8):
        top = jnp.where(sub == k, full[k], top)
    out = list(rows)
    out[p] = top
    for i, c in rest.items():
        t = [c[j] * full[j] for j in range(8)]
        s = ((t[0] + t[1]) + (t[2] + t[3])) + ((t[4] + t[5]) + (t[6] + t[7]))
        out[i] = jnp.where(inside, 0.0, rows[i]) - s
    return out


def inverse_128(a):
    lane = lax.broadcasted_iota(jnp.int32, (8, 128), 1)
    sub = lax.broadcasted_iota(jnp.int32, (8, 128), 0)

    def some(_, rows):
        for p in range(PER):
            rows = eliminate_eight(rows, p, lane, sub)
        rows = [pltpu.roll(v, 128 - 8 * PER, 1) for v in rows]
        return tuple(rows[PER:] + rows[:PER])

    rows = lax.fori_loop(0, 16 // PER, some, tuple(a[8 * i : 8 * i + 8, :] for i in range(16)))
    return jnp.concatenate(rows, axis=0)


def contract(a, b, dims):
    return lax.dot_general(a, b, (dims, ((), ())), precision=HI, preferred_element_type=F32)


def dot(a, b):
    return contract(a, b, ((1,), (0,)))


def dot_nt(a, b):
    return contract(a, b, ((1,), (1,)))


def dot_tn(a, b):
    return contract(a, b, ((0,), (0,)))


def inverse_in_place(ref):
    n, b = ref.shape[0], 128
    block_of_row = lax.broadcasted_iota(jnp.int32, (n, 1), 0) // b

    def step(i, _):
        o = pl.multiple_of(i * b, b)
        pivot = inverse_128(ref[pl.ds(o, b), pl.ds(o, b)])
        across = dot(pivot, ref[pl.ds(o, b), :])
        down = jnp.where(block_of_row == i, 0.0, ref[:, pl.ds(o, b)])
        rest = ref[...] - dot(down, across)
        left = -dot(down, pivot)
        ref[...] = rest
        ref[pl.ds(o, b), :] = across
        ref[:, pl.ds(o, b)] = left
        ref[pl.ds(o, b), pl.ds(o, b)] = pivot
        return 0

    lax.fori_loop(0, n // b, step, 0)


def half_inverse(corner, below, inv_ref, low_ref, below_ref):
    inv_ref[...] = corner
    inverse_in_place(inv_ref)
    below_ref[...] = below
    low_ref[...] = dot(below, inv_ref[...])


def whole_inverse(corner, inv, low, below, out_ref, work):
    h = HALF
    work[...] = corner - dot_nt(low, below)
    inverse_in_place(work)
    e = dot(work[...], low)
    out_ref[h : 2 * h, h : 2 * h] = work[...]
    out_ref[h : 2 * h, 0:h] = -e
    out_ref[0:h, h : 2 * h] = -e.T
    out_ref[0:h, 0:h] = inv + dot_tn(low, e)


def half_one_kernel(mine, other, *outs):
    s = mine[...] + other[...]
    half_inverse(s[0:HALF], s[HALF : 2 * HALF], *outs)


def whole_one_kernel(mine, other, inv, low, below, out, work):
    whole_inverse(mine[...] + other[...], inv[...], low[...], below[...], out, work)


def half_two_kernel(where, mine, other, *outs):
    first = where[0] == 0
    half_inverse(
        jnp.where(first, mine[...], other[...]), jnp.where(first, other[...], mine[...]), *outs
    )


def whole_two_kernel(where, mine, other, inv, low, below, out, work):
    first = where[0] == 0
    corner = jnp.concatenate(
        [jnp.where(first, mine[...], other[...]), jnp.where(first, other[...], mine[...])], axis=0
    )
    whole_inverse(corner, inv[...], low[...], below[...], out, work)


SQUARE = jax.ShapeDtypeStruct((HALF, HALF), F32)
HALF_COST = 16 * 10**9


def pick_rows(idx_ref, start, src, dst, count):
    def eight(g, _):
        base = g * 8
        got = [src[pl.ds(idx_ref[start + base + i], 1), :] for i in range(8)]
        dst[pl.ds(pl.multiple_of(base, 8), 8), :] = jnp.concatenate(got, axis=0)
        return 0

    lax.fori_loop(0, count // 8, eight, 0)


def gather_kernel(idx_ref, a_ref, *refs):
    parts, whole, rows = refs[: 2 * PARTS], refs[2 * PARTS : 2 * PARTS + 2], refs[-1]
    pick_rows(idx_ref, 0, a_ref, rows, EDGE)
    h = parts[0].shape[0]
    for k in range(0, EDGE, 128):
        t = rows[k : k + 128, :].T
        lo = k % HALF
        for side in range(2):
            piece = t[side * h : (side + 1) * h, :]
            parts[2 * (k // HALF) + side][:, lo : lo + 128] = piece
            whole[side][:, k : k + 128] = piece


def select_kernel(start, count, idx_ref, *refs):
    pieces, o_ref, stack = refs[:8], refs[8], refs[9]
    h = pieces[0].shape[0]
    for k, piece in enumerate(pieces):
        stack[k * h : (k + 1) * h, :] = piece[...]
    pick_rows(idx_ref, start, stack, o_ref, count)


def column_of(row, n):
    return jnp.broadcast_to(row, (128, n)).T


def half_of(parity):
    return pl.ds(pl.multiple_of(parity * HALF, HALF), HALF)


def middle_kernel(where, inv, t_own, t_sib, m_ref, mh_ref, ab_ref, d_ref, x_all, y_one):
    parity = where[0]
    x_all[:, half_of(parity)] = t_own[0:IFACE, :]
    x_all[:, half_of(1 - parity)] = t_sib[0:IFACE, :]
    y_one[...] = jnp.where(parity == 1, t_own[IFACE:EDGE, :], t_sib[IFACE:EDGE, :])
    m_ref[...] = dot(inv[...], x_all[...])
    mh_ref[...] = m_ref[half_of(parity), :]
    y_zero = jnp.where(parity == 0, t_own[IFACE:EDGE, :], 0.0)
    ab_ref[...] = y_zero - dot_tn(t_own[0:IFACE, :], m_ref[:, 0:HALF])
    o = pl.multiple_of(parity * 128, 128)
    part = x_all[:, pl.ds(pl.multiple_of(HALF + parity * 128, 128), 128)]
    d_ref[...] = y_one[pl.ds(o, 128), :] - dot_tn(part, m_ref[:, HALF:IFACE])


def split(v):
    high = v.astype(BF16)
    return high, (v - high.astype(F32)).astype(BF16)


def three(a, b, dims=((1,), (0,))):
    def one(x, y):
        return lax.dot_general(x, y, (dims, ((), ())), preferred_element_type=F32)

    return one(a[0], b[0]) + (one(a[0], b[1]) + one(a[1], b[0]))


def side_kernel(where, inv, m, keep, whole_a, whole_b, gt_ref, w_ref):
    h = whole_a.shape[0]
    mask = jnp.tile(column_of(keep[...], 2 * h), (1, IFACE // 128))
    m2, inv2 = split(m[...]), split(inv[...])
    mine = half_of(where[0])
    for side, whole in enumerate((whole_a, whole_b)):
        rows = slice(side * h, (side + 1) * h)
        pi = split(whole[:, 0:IFACE])
        w_ref[rows, :] = three(pi, inv2) * mask[rows]
        gt_ref[rows, :] = -three(pi, m2)
        gt_ref[rows, mine] = gt_ref[rows, mine] + whole[:, IFACE:EDGE]
        gt_ref[rows, :] = gt_ref[rows, :] * mask[rows]


def last_kernel(where, inv, m_ref, mz, mz_sib, gt, w1t, a_ref, keep4, keep_col, *refs):
    n_in = 2 * PARTS + 16
    ins, out = refs[:n_in], refs[n_in]
    edges, hi, lo, block, m_far, in_sems, out_sems = refs[n_in + 1 :]
    parity, quad, col = where[0], where[1], where[2]
    w = gt.shape[0]
    child = COLS * w
    copies = []

    def load(src, dst):
        c = pltpu.make_async_copy(src, dst, in_sems.at[len(copies)])
        c.start()
        copies.append(c)

    for m in range(2):
        for k in range(PARTS):
            load(ins[PARTS * m + k], edges.at[pl.ds(m * child, child), pl.ds(k * HALF, HALF)])
    for m in range(2):
        for k in range(8):
            o = (2 + m) * child + k * (w // 2)
            load(ins[2 * PARTS + 8 * m + k], edges.at[pl.ds(o, w // 2), :])

    m_far[half_of(parity), :] = mz[...]
    m_far[half_of(1 - parity), :] = mz_sib[...]
    nt = ((1,), (1,))
    vt = three(split(gt[...]), split(inv[...]))
    vt2 = split(vt)
    ut = w1t[...] - three(vt2, split(m_ref[...]), nt)
    far = -three(vt2, split(m_far[...]), nt)
    u, f, v = split(ut.T), split(far.T), split(vt.T)
    for ref, part in ((hi, 0), (lo, 1)):
        for k in range(4):
            ref[k, 0:IFACE, :] = (u if k < 2 else f)[part]
        for k in range(2):
            half = v[part][k * HALF : (k + 1) * HALF]
            same = k ^ parity
            ref[same, IFACE:EDGE, :] = half
            ref[same + 2, IFACE:EDGE, :] = half
    for c in copies:
        c.wait()

    def store(i):
        m, r = i // COLS, i % COLS
        o = (quad ^ m) * child + ((col + r) % COLS) * w
        return pltpu.make_async_copy(
            block.at[i % 2], out.at[pl.ds(pl.multiple_of(o, w), w), :], out_sems.at[i % 2]
        )

    def one(i, _):
        m, r = i // COLS, i % COLS

        @pl.when(i >= 2)
        def _():
            store(i - 2).wait()

        e = split(edges[pl.ds(pl.multiple_of(i * w, w), w), :])
        total = -three(e, (hi[m], lo[m]))
        here = pl.ds(pl.multiple_of(((col + r) % COLS) * w, w), w)
        mask = jnp.tile(column_of(keep4[pl.ds(m, 1), here], w), (1, w // 128))
        block[i % 2] = total * mask

        @pl.when(m == 0)
        def _():
            block[i % 2] = block[i % 2] + a_ref[here, :] * keep_col[...] * mask

        store(i).start()
        return 0

    lax.fori_loop(0, 4 * COLS, one, 0)
    store(4 * COLS - 2).wait()
    store(4 * COLS - 1).wait()


def swapped(shard, apart):
    n = lax.axis_size("box")
    return lax.ppermute(shard, "box", [(i, i ^ apart) for i in range(n)])


def shifted(shard, by):
    return lax.ppermute(shard, "col", [((i + by) % COLS, i) for i in range(COLS)])


def after(values, *others):
    return lax.optimization_barrier((values, others))[0]


def around(top, bottom):
    right_top, left_bottom = shifted(top, 1), shifted(bottom, -1)
    right_bottom, left_top = shifted(bottom, 1), shifted(top, -1)
    return (top, bottom, right_top, right_bottom, left_top, left_bottom), (right_top, left_bottom)


def farther(near, *done):
    top, bottom, right_top, right_bottom, left_top, left_bottom = near
    up, down = after((right_top, left_bottom), *done)
    far_top, far_bottom = shifted(up, 1), shifted(down, -1)
    return top, bottom, right_top, right_bottom, far_top, far_bottom, left_top, left_bottom


def select(start, count, relative, pieces):
    rows = 8 * pieces[0].shape[0]
    return call(
        functools.partial(select_kernel, start, count),
        (shape(count, HALF), shape(rows, HALF)),
        1,
        8,
        3 * 10**9,
        8 * rows * HALF,
    )(relative, *pieces)


def merged(child_maps, iface_one, iface_two):
    a = child_maps[0]
    boundary, w = a.shape
    box, col = lax.axis_index("box"), lax.axis_index("col")
    parity = box % 2
    own_one = iface_one[0]
    group = lax.dynamic_index_in_dim(iface_two, box // 2, 0, keepdims=False)
    own_two = lax.dynamic_slice_in_dim(group, parity * HALF, HALF) - parity * boundary
    points = jnp.concatenate([own_one, own_two])

    h = w // 2
    *parts, whole_a, whole_b = call(
        gather_kernel,
        (shape(h, HALF),) * (2 * PARTS) + (shape(h, EDGE),) * 2,
        1,
        1,
        0,
        4 * boundary * w,
        [pltpu.VMEM((EDGE, w), F32)],
    )(points, a)
    near0, first0 = around(parts[0], parts[1])
    part0 = farther(near0)
    relative = (points - col * w) % boundary
    where = jnp.stack([parity, box % 4, col]).astype(jnp.int32)
    near1, first1 = around(*after((parts[2], parts[3]), *first0))
    part1 = farther(near1)
    far_a, far_b = swapped(whole_a, 2), swapped(whole_b, 2)

    t0, stack0 = select(0, IFACE, relative, part0)
    t0, t0_sib = after((t0, swapped(t0, 1)), *first1)
    half = call(half_one_kernel, (SQUARE,) * 3, 0, 2, HALF_COST, 10**6)(t0, t0_sib)

    near2, first2 = around(*after((parts[4], parts[5]), *first1))
    part2 = farther(near2)
    t1, stack1 = select(HALF, HALF, relative, after(part1, half[0]))
    t1, t1_sib = after((t1, swapped(t1, 1)), *first2)
    inv_one = call(
        whole_one_kernel, shape(IFACE, IFACE), 0, 5, HALF_COST, 10**6,
        [pltpu.VMEM((HALF, HALF), F32)],
    )(t1, t1_sib, *half)

    nearz, _ = around(*after((far_a, far_b), *first2))
    t2, stack2 = select(0, EDGE, relative, after(part2, inv_one))
    m, m_half, ab, d = call(
        middle_kernel,
        (shape(IFACE, IFACE), shape(HALF, IFACE), SQUARE, shape(128, HALF)),
        1,
        3,
        5 * 10**9,
        2**22,
        [pltpu.VMEM((IFACE, IFACE), F32), pltpu.VMEM((HALF, HALF), F32)],
    )(where, inv_one, t2, swapped(t2, 1))

    matches = jnp.arange(boundary, dtype=jnp.int32)[None, :] == points[:, None]
    keep = 1.0 - jnp.sum(matches.astype(F32), axis=0)
    keep_col = lax.dynamic_slice_in_dim(keep, col * w, w)[None, :]
    keep4 = jnp.stack([keep, swapped(keep, 1), swapped(keep, 2), swapped(keep, 3)])

    ab_far = swapped(ab, 2)
    gt, w1t = call(
        side_kernel, (shape(w, IFACE),) * 2, 1, 5, 3 * 10**9, 2**22
    )(where, inv_one, m, keep_col, whole_a, whole_b)
    partz = farther(nearz, gt)
    ab = ab + ab_far
    ab_sib = swapped(ab, 1)
    d = after(d, ab_far)
    d = d + swapped(d, 2)
    d_sib = swapped(d, 1)
    half = call(half_two_kernel, (SQUARE,) * 3, 1, 2, HALF_COST, 10**6)(where, ab, ab_sib)
    inv_two = call(
        whole_two_kernel, shape(IFACE, IFACE), 1, 5, HALF_COST, 10**6,
        [pltpu.VMEM((HALF, HALF), F32)],
    )(where, d, d_sib, *half)

    m_far = swapped(after(m_half, d), 2)
    stacks = (stack0, stack1, stack2)
    stacks_sib = [swapped(v, 1) for v in stacks]
    partz_sib = [swapped(v, 1) for v in partz]
    out = pl.pallas_call(
        last_kernel,
        name="last",
        out_shape=shape(COLS * boundary, w),
        in_specs=[SMEM] + [VMEM] * 9 + [ANY] * (2 * PARTS + 16),
        out_specs=ANY,
        scratch_shapes=[
            pltpu.VMEM((4 * boundary, EDGE), F32),
            pltpu.VMEM((4, EDGE, w), BF16),
            pltpu.VMEM((4, EDGE, w), BF16),
            pltpu.VMEM((2, w, w), F32),
            pltpu.VMEM((IFACE, IFACE), F32),
            pltpu.SemaphoreType.DMA((2 * PARTS + 16,)),
            pltpu.SemaphoreType.DMA((2,)),
        ],
        cost_estimate=pl.CostEstimate(flops=10**10, bytes_accessed=3 * 10**7, transcendentals=0),
        compiler_params=pltpu.CompilerParams(vmem_limit_bytes=56 * 2**20),
    )(
        where, inv_two, m, m_far, swapped(m_far, 1), gt, w1t, a, keep4, keep_col,
        *stacks, *stacks_sib, *partz, *partz_sib,
    )
    return out[None]


def solution(mesh):
    return jax.shard_map(
        merged,
        mesh=mesh,
        in_specs=(P("box", None, "col"), P("box", None), P()),
        out_specs=P("box", None, "col"),
        check_vma=False,
    )
```

```python
import functools

import jax
import jax.numpy as jnp
from jax import lax
from jax.experimental import pallas as pl
from jax.experimental.pallas import tpu as pltpu
from jax.sharding import PartitionSpec as P

F32 = jnp.float32
BF16 = jnp.bfloat16
HI = lax.Precision.HIGHEST
COLS = 4
IFACE = 512
HALF = 256
EDGE = IFACE + HALF
PARTS = EDGE // HALF


PER = 4

VMEM = pl.BlockSpec(memory_space=pltpu.VMEM)
SMEM = pl.BlockSpec(memory_space=pltpu.SMEM)
ANY = pl.BlockSpec(memory_space=pl.ANY)


def call(body, outs, n_smem, n_in, flops, nbytes, scratch=()):
    return pl.pallas_call(
        body,
        out_shape=outs,
        in_specs=[SMEM] * n_smem + [VMEM] * n_in,
        out_specs=jax.tree.map(lambda _: VMEM, outs),
        scratch_shapes=scratch,
        cost_estimate=pl.CostEstimate(flops=flops, bytes_accessed=nbytes, transcendentals=0),
        compiler_params=pltpu.CompilerParams(vmem_limit_bytes=20 * 2**20),
    )


def shape(*dims):
    return jax.ShapeDtypeStruct(dims, F32)


def lane_of(v, j):
    return jnp.broadcast_to(v[:, j : j + 1], v.shape)


def row_of(v, r):
    return jnp.broadcast_to(v[r : r + 1, :], v.shape)


def eliminate_eight(rows, p, lane, sub):
    off = 8 * p
    full = [row_of(rows[p], k) for k in range(8)]
    e = {(k, j): lane_of(full[k], off + j) for k in range(8) for j in range(k, 8)}
    rest = {i: [lane_of(rows[i], off + j) for j in range(8)] for i in range(16) if i != p}
    inside = (lane >= off) & (lane < off + 8)
    full = [jnp.where(inside, jnp.where(lane == off + k, 1.0, 0.0), full[k]) for k in range(8)]
    low, inv = {}, []
    for k in range(8):
        inv.append(1.0 / e[k, k])
        for r in range(k + 1, 8):
            low[r, k] = e[k, r] * inv[k]
            full[r] = full[r] - low[r, k] * full[k]
        for r in range(k + 1, 8):
            for j in range(r, 8):
                e[r, j] = e[r, j] - low[r, k] * e[k, j]
    full = [full[k] * inv[k] for k in range(8)]
    for k in range(7, 0, -1):
        for r in range(k):
            full[r] = full[r] - low[k, r] * full[k]
    top = full[0]
    for k in range(1, 8):
        top = jnp.where(sub == k, full[k], top)
    out = list(rows)
    out[p] = top
    for i, c in rest.items():
        t = [c[j] * full[j] for j in range(8)]
        s = ((t[0] + t[1]) + (t[2] + t[3])) + ((t[4] + t[5]) + (t[6] + t[7]))
        out[i] = jnp.where(inside, 0.0, rows[i]) - s
    return out


def inverse_128(a):
    lane = lax.broadcasted_iota(jnp.int32, (8, 128), 1)
    sub = lax.broadcasted_iota(jnp.int32, (8, 128), 0)

    def some(_, rows):
        for p in range(PER):
            rows = eliminate_eight(rows, p, lane, sub)
        rows = [pltpu.roll(v, 128 - 8 * PER, 1) for v in rows]
        return tuple(rows[PER:] + rows[:PER])

    rows = lax.fori_loop(0, 16 // PER, some, tuple(a[8 * i : 8 * i + 8, :] for i in range(16)))
    return jnp.concatenate(rows, axis=0)


def contract(a, b, dims):
    return lax.dot_general(a, b, (dims, ((), ())), precision=HI, preferred_element_type=F32)


def dot(a, b):
    return contract(a, b, ((1,), (0,)))


def dot_nt(a, b):
    return contract(a, b, ((1,), (1,)))


def dot_tn(a, b):
    return contract(a, b, ((0,), (0,)))


def inverse_in_place(ref):
    n, b = ref.shape[0], 128
    block_of_row = lax.broadcasted_iota(jnp.int32, (n, 1), 0) // b

    def step(i, _):
        o = pl.multiple_of(i * b, b)
        pivot = inverse_128(ref[pl.ds(o, b), pl.ds(o, b)])
        across = dot(pivot, ref[pl.ds(o, b), :])
        down = jnp.where(block_of_row == i, 0.0, ref[:, pl.ds(o, b)])
        rest = ref[...] - dot(down, across)
        left = -dot(down, pivot)
        ref[...] = rest
        ref[pl.ds(o, b), :] = across
        ref[:, pl.ds(o, b)] = left
        ref[pl.ds(o, b), pl.ds(o, b)] = pivot
        return 0

    lax.fori_loop(0, n // b, step, 0)


def by_rows(n, body):
    def one(i, _):
        body(pl.ds(pl.multiple_of(i * 128, 128), 128))
        return 0

    lax.fori_loop(0, n // 128, one, 0)


def half_inverse(corner, below, inv_ref, low_ref, below_ref):
    inv_ref[...] = corner
    inverse_in_place(inv_ref)
    below_ref[...] = below

    def some(rows):
        low_ref[rows, :] = dot(below_ref[rows, :], inv_ref[...])

    by_rows(HALF, some)


def whole_inverse(corner, inv, low, below, out_ref, work):
    h = HALF
    work[...] = corner

    def schur(rows):
        work[rows, :] = work[rows, :] - dot_nt(low[rows, :], below[...])

    by_rows(h, schur)
    inverse_in_place(work)

    def lower(rows):
        out_ref[pl.ds(h + rows.start, 128), 0:h] = -dot(work[rows, :], low[...])

    by_rows(h, lower)

    def upper(rows):
        out_ref[rows, 0:h] = inv[rows, :] - dot_tn(low[:, rows], out_ref[h : 2 * h, 0:h])

    by_rows(h, upper)
    out_ref[h : 2 * h, h : 2 * h] = work[...]
    out_ref[0:h, h : 2 * h] = out_ref[h : 2 * h, 0:h].T


def half_one_kernel(mine, other, *outs):
    s = mine[...] + other[...]
    half_inverse(s[0:HALF], s[HALF : 2 * HALF], *outs)


def whole_one_kernel(mine, other, inv, low, below, out, work):
    whole_inverse(mine[...] + other[...], inv, low, below, out, work)


def half_two_kernel(where, mine, other, *outs):
    first = where[0] == 0
    half_inverse(
        jnp.where(first, mine[...], other[...]), jnp.where(first, other[...], mine[...]), *outs
    )


def whole_two_kernel(where, mine, other, inv, low, below, out, work):
    first = where[0] == 0
    corner = jnp.concatenate(
        [jnp.where(first, mine[...], other[...]), jnp.where(first, other[...], mine[...])], axis=0
    )
    whole_inverse(corner, inv, low, below, out, work)


SQUARE = jax.ShapeDtypeStruct((HALF, HALF), F32)
HALF_COST = 16 * 10**9


def pick_rows(idx_ref, start, src, dst, count):
    def eight(g, _):
        base = g * 8
        got = [src[pl.ds(idx_ref[start + base + i], 1), :] for i in range(8)]
        dst[pl.ds(pl.multiple_of(base, 8), 8), :] = jnp.concatenate(got, axis=0)
        return 0

    lax.fori_loop(0, count // 8, eight, 0)


def gather_kernel(idx_ref, a_ref, list_ref, *refs):
    parts, whole, rows = refs[:PARTS], refs[PARTS], refs[PARTS + 1]
    pick_rows(idx_ref, 0, a_ref, rows, EDGE)
    w = whole.shape[0]
    point = lax.broadcasted_iota(jnp.int32, (w, 1), 0) + lax.axis_index("col") * w
    hits = jnp.sum((list_ref[...] == point).astype(F32), axis=1, keepdims=True)
    keep = 1.0 - hits
    for k in range(0, EDGE, 128):
        t = rows[k : k + 128, :].T
        lo = k % HALF
        parts[k // HALF][:, lo : lo + 128] = t
        whole[:, k : k + 128] = t * keep


def select_kernel(start, count, idx_ref, *refs):
    pieces, o_ref, stack = refs[:COLS], refs[COLS], refs[COLS + 1]
    w = pieces[0].shape[0]
    for k, piece in enumerate(pieces):
        stack[k * w : (k + 1) * w, :] = piece[...]
    pick_rows(idx_ref, start, stack, o_ref, count)


def column_of(row, n):
    return jnp.broadcast_to(row, (128, n)).T


def half_of(parity):
    return pl.ds(pl.multiple_of(parity * HALF, HALF), HALF)


def middle_kernel(where, inv, t_own, t_sib, m_ref, mh_ref, ab_ref, d_ref, x_all, y_one):
    parity = where[0]
    x_all[:, half_of(parity)] = t_own[0:IFACE, :]
    x_all[:, half_of(1 - parity)] = t_sib[0:IFACE, :]
    y_one[...] = jnp.where(parity == 1, t_own[IFACE:EDGE, :], t_sib[IFACE:EDGE, :])

    def rows_of_m(rows):
        m_ref[rows, :] = dot(inv[rows, :], x_all[...])

    by_rows(IFACE, rows_of_m)
    mh_ref[...] = m_ref[half_of(parity), :]
    y_zero = jnp.where(parity == 0, t_own[IFACE:EDGE, :], 0.0)
    ab_ref[...] = y_zero

    def rows_of_ab(rows):
        ab_ref[rows, :] = ab_ref[rows, :] - dot_tn(t_own[0:IFACE, rows], m_ref[:, 0:HALF])

    by_rows(HALF, rows_of_ab)
    o = pl.multiple_of(parity * 128, 128)
    part = x_all[:, pl.ds(pl.multiple_of(HALF + parity * 128, 128), 128)]
    d_ref[...] = y_one[pl.ds(o, 128), :] - dot_tn(part, m_ref[:, HALF:IFACE])


def split(v):
    high = v.astype(BF16)
    return high, (v - high.astype(F32)).astype(BF16)


def three(a, b, dims=((1,), (0,))):
    def one(x, y):
        return lax.dot_general(x, y, (dims, ((), ())), preferred_element_type=F32)

    return one(a[0], b[0]) + (one(a[0], b[1]) + one(a[1], b[0]))


def side_kernel(where, inv, m, whole, gt_ref, w_ref):
    m2, inv2 = split(m[...]), split(inv[...])
    mine = half_of(where[0])

    def some(rows):
        pi = split(whole[rows, 0:IFACE])
        w_ref[rows, :] = three(pi, inv2)
        gt_ref[rows, :] = -three(pi, m2)
        gt_ref[rows, mine] = gt_ref[rows, mine] + whole[rows, IFACE:EDGE]

    by_rows(whole.shape[0], some)


def last_kernel(where, inv, m_ref, mz, mz_sib, gt, w1t, a_ref, keep2, keep_col, *refs):
    n_in = 2 * PARTS + 2 * (COLS + 1)
    ins, out = refs[:n_in], refs[n_in]
    edges, both, block, m_far, vt_ref, ut_ref, ft_ref, in_sems, out_sems = refs[n_in + 1 :]
    parity, quad, col = where[0], where[1], where[2]
    w = gt.shape[0]
    child = COLS * w
    copies = [[], [], [], []]

    def load(m, k, src, dst):
        c = pltpu.make_async_copy(src, dst, in_sems.at[m, k])
        c.start()
        copies[m].append(c)

    for m in range(2):
        for k in range(PARTS):
            dst = edges.at[pl.ds(m * child, child), pl.ds(k * HALF, HALF)]
            load(m, k, ins[PARTS * m + k], dst)
    for m in range(2):
        start = (2 + m) * child
        for k in range(COLS + 1):
            piece = ins[2 * PARTS + (COLS + 1) * m + k]
            load(2 + m, k, piece, edges.at[pl.ds(start, piece.shape[0]), :])
            start += piece.shape[0]

    m_far[half_of(parity), :] = mz[...]
    m_far[half_of(1 - parity), :] = mz_sib[...]
    nt = ((1,), (1,))
    inv2, near2, far2 = split(inv[...]), split(m_ref[...]), split(m_far[...])

    def some(rows):
        vt = three(split(gt[rows, :]), inv2)
        vt2 = split(vt)
        vt_ref[rows, :] = vt
        ut_ref[rows, :] = w1t[rows, :] - three(vt2, near2, nt)
        ft_ref[rows, :] = -three(vt2, far2, nt)

    by_rows(w, some)
    u, f, v = split(ut_ref[...].T), split(ft_ref[...].T), split(vt_ref[...].T)
    for part in range(2):
        lanes = slice(part * w, (part + 1) * w)
        for k in range(4):
            both[k, 0:IFACE, lanes] = (u if k < 2 else f)[part]
        for k in range(2):
            half = v[part][k * HALF : (k + 1) * HALF]
            same = k ^ parity
            both[same, IFACE:EDGE, lanes] = half
            both[same + 2, IFACE:EDGE, lanes] = half

    def store(i):
        m, r = i // COLS, i % COLS
        o = (quad ^ m) * child + ((col + r) % COLS) * w
        return pltpu.make_async_copy(
            block.at[i % 2], out.at[pl.ds(pl.multiple_of(o, w), w), :], out_sems.at[i % 2]
        )

    def one(i, _):
        m, r = i // COLS, i % COLS
        for k in range(4):

            @pl.when(i == k * COLS)
            def _():
                for c in copies[k]:
                    c.wait()

        @pl.when(i >= 2)
        def _():
            store(i - 2).wait()

        high, low = split(edges[pl.ds(pl.multiple_of(i * w, w), w), :])
        wide = jnp.dot(high, both[m], preferred_element_type=F32)
        total = wide[:, 0:w] + (
            wide[:, w : 2 * w] + jnp.dot(low, both[m, :, 0:w], preferred_element_type=F32)
        )
        block[i % 2] = -total

        @pl.when(m < 2)
        def _():
            here = pl.ds(pl.multiple_of(((col + r) % COLS) * w, w), w)
            mask = jnp.tile(column_of(keep2[pl.ds(jnp.minimum(m, 1), 1), here], w), (1, w // 128))
            own = jnp.where(m == 0, keep_col[...], 0.0)
            block[i % 2] = (block[i % 2] + a_ref[here, :] * own) * mask

        store(i).start()
        return 0

    lax.fori_loop(0, 4 * COLS, one, 0)
    store(4 * COLS - 2).wait()
    store(4 * COLS - 1).wait()


def swapped(shard, apart):
    n = lax.axis_size("box")
    return lax.ppermute(shard, "box", [(i, i ^ apart) for i in range(n)])


def shifted(shard, by):
    return lax.ppermute(shard, "col", [((i + by) % COLS, i) for i in range(COLS)])


def after(values, *others):
    return lax.optimization_barrier((values, others))[0]


def around(own, forward):
    right, left = shifted(own, 1), shifted(own, -1)
    return (own, right, left), (right if forward == 1 else left)


def farther(near, forward):
    own, right, left = near
    far = shifted(right if forward == 1 else left, forward)
    return own, right, far, left


def farther_both(near, done):
    own, right, left = near
    h = own.shape[0] // 2
    top, bottom = after((right[:h], left[h:]), done)
    far = shifted(top, 1), shifted(bottom, -1)
    return own, right, *far, left


def select(start, count, relative, pieces):
    rows = COLS * pieces[0].shape[0]
    return call(
        functools.partial(select_kernel, start, count),
        (shape(count, HALF), shape(rows, HALF)),
        1,
        COLS,
        3 * 10**9,
        8 * rows * HALF,
    )(relative, *pieces)


def merged(child_maps, iface_one, iface_two):
    a = child_maps[0]
    boundary, w = a.shape
    box, col = lax.axis_index("box"), lax.axis_index("col")
    parity = box % 2
    own_one = iface_one[0]
    group = lax.dynamic_index_in_dim(iface_two, box // 2, 0, keepdims=False)
    own_two = lax.dynamic_slice_in_dim(group, parity * HALF, HALF) - parity * boundary
    points = jnp.concatenate([own_one, own_two])

    *parts, whole = call(
        gather_kernel,
        (shape(w, HALF),) * PARTS + (shape(w, EDGE),),
        1,
        2,
        0,
        4 * boundary * w,
        [pltpu.VMEM((EDGE, w), F32)],
    )(points, a, points[None, :])
    near0, first0 = around(parts[0], 1)
    part0 = farther(near0, 1)
    relative = (points - col * w) % boundary
    where = jnp.stack([parity, box % 4, col]).astype(jnp.int32)
    near1, first1 = around(after(parts[1], first0), -1)
    part1 = farther(near1, -1)
    far = swapped(whole, 2)
    matches = jnp.arange(boundary, dtype=jnp.int32)[None, :] == points[:, None]
    keep = 1.0 - jnp.sum(matches.astype(F32), axis=0)
    keep_col = lax.dynamic_slice_in_dim(keep, col * w, w)[None, :]
    keep2 = jnp.stack([keep, swapped(keep, 1)])

    t0, stack0 = select(0, IFACE, relative, part0)
    t0, t0_sib, where, keep2, keep_col = after(
        (t0, swapped(t0, 1), where, keep2, keep_col), first1
    )
    half = call(half_one_kernel, (SQUARE,) * 3, 0, 2, HALF_COST, 10**6)(t0, t0_sib)

    near2, first2 = around(after(parts[2], first1), 1)
    part2 = farther(near2, 1)
    t1, stack1 = select(HALF, HALF, relative, after(part1, half[0]))
    t1, t1_sib = after((t1, swapped(t1, 1)), first2)
    inv_one = call(
        whole_one_kernel, shape(IFACE, IFACE), 0, 5, HALF_COST, 10**6,
        [pltpu.VMEM((HALF, HALF), F32)],
    )(t1, t1_sib, *half)

    nearz, _ = around(after(far, first2), -1)
    t2, stack2 = select(0, EDGE, relative, after(part2, inv_one))
    m, m_half, ab, d = call(
        middle_kernel,
        (shape(IFACE, IFACE), shape(HALF, IFACE), SQUARE, shape(128, HALF)),
        1,
        3,
        5 * 10**9,
        2**22,
        [pltpu.VMEM((IFACE, IFACE), F32), pltpu.VMEM((HALF, HALF), F32)],
    )(where, inv_one, t2, swapped(t2, 1))

    ab_far = swapped(ab, 2)
    gt, w1t = call(
        side_kernel, (shape(w, IFACE),) * 2, 1, 3, 3 * 10**9, 2**22
    )(where, inv_one, m, whole)
    partz = farther_both(nearz, gt)
    ab = ab + ab_far
    ab_sib = swapped(ab, 1)
    d = after(d, ab_far)
    d = d + swapped(d, 2)
    d_sib = swapped(d, 1)
    half = call(half_two_kernel, (SQUARE,) * 3, 1, 2, HALF_COST, 10**6)(where, ab, ab_sib)
    inv_two = call(
        whole_two_kernel, shape(IFACE, IFACE), 1, 5, HALF_COST, 10**6,
        [pltpu.VMEM((HALF, HALF), F32)],
    )(where, d, d_sib, *half)

    m_far = swapped(after(m_half, d), 2)
    stacks = (stack0, stack1, stack2)
    stacks_sib = [swapped(v, 1) for v in stacks]
    partz_sib = [swapped(v, 1) for v in partz]
    out = pl.pallas_call(
        last_kernel,
        name="last",
        out_shape=shape(COLS * boundary, w),
        in_specs=[SMEM] + [VMEM] * 9 + [ANY] * (2 * PARTS + 2 * (COLS + 1)),
        out_specs=ANY,
        scratch_shapes=[
            pltpu.VMEM((4 * boundary, EDGE), F32),
            pltpu.VMEM((4, EDGE, 2 * w), BF16),
            pltpu.VMEM((2, w, w), F32),
            pltpu.VMEM((IFACE, IFACE), F32),
            pltpu.VMEM((w, IFACE), F32),
            pltpu.VMEM((w, IFACE), F32),
            pltpu.VMEM((w, IFACE), F32),
            pltpu.SemaphoreType.DMA((4, COLS + 1)),
            pltpu.SemaphoreType.DMA((2,)),
        ],
        cost_estimate=pl.CostEstimate(flops=10**10, bytes_accessed=3 * 10**7, transcendentals=0),
        compiler_params=pltpu.CompilerParams(vmem_limit_bytes=48 * 2**20),
    )(
        where, inv_two, m, m_far, swapped(m_far, 1), gt, w1t, a, keep2, keep_col,
        *stacks, *stacks_sib, *partz, *partz_sib,
    )
    return out[None]


def solution(mesh):
    return jax.shard_map(
        merged,
        mesh=mesh,
        in_specs=(P("box", None, "col"), P("box", None), P()),
        out_specs=P("box", None, "col"),
        check_vma=False,
    )
```

```python
import functools

import jax
import jax.numpy as jnp
from jax import lax
from jax.experimental import pallas as pl
from jax.experimental.pallas import tpu as pltpu
from jax.sharding import PartitionSpec as P

F32 = jnp.float32
BF16 = jnp.bfloat16
HI = lax.Precision.HIGHEST
COLS = 4
IFACE = 512
HALF = 256
EDGE = IFACE + HALF
PARTS = EDGE // HALF


PER = 4

VMEM = pl.BlockSpec(memory_space=pltpu.VMEM)
SMEM = pl.BlockSpec(memory_space=pltpu.SMEM)
ANY = pl.BlockSpec(memory_space=pl.ANY)


def call(body, outs, n_smem, n_in, flops, nbytes, scratch=()):
    return pl.pallas_call(
        body,
        out_shape=outs,
        in_specs=[SMEM] * n_smem + [VMEM] * n_in,
        out_specs=jax.tree.map(lambda _: VMEM, outs),
        scratch_shapes=scratch,
        cost_estimate=pl.CostEstimate(flops=flops, bytes_accessed=nbytes, transcendentals=0),
        compiler_params=pltpu.CompilerParams(vmem_limit_bytes=20 * 2**20),
    )


def shape(*dims):
    return jax.ShapeDtypeStruct(dims, F32)


def lane_of(v, j):
    return jnp.broadcast_to(v[:, j : j + 1], v.shape)


def row_of(v, r):
    return jnp.broadcast_to(v[r : r + 1, :], v.shape)


def eliminate_eight(rows, p, lane, sub):
    off = 8 * p
    full = [row_of(rows[p], k) for k in range(8)]
    e = {(k, j): lane_of(full[k], off + j) for k in range(8) for j in range(k, 8)}
    rest = {i: [lane_of(rows[i], off + j) for j in range(8)] for i in range(16) if i != p}
    inside = (lane >= off) & (lane < off + 8)
    full = [jnp.where(inside, jnp.where(lane == off + k, 1.0, 0.0), full[k]) for k in range(8)]
    low, inv = {}, []
    for k in range(8):
        inv.append(1.0 / e[k, k])
        for r in range(k + 1, 8):
            low[r, k] = e[k, r] * inv[k]
            full[r] = full[r] - low[r, k] * full[k]
        for r in range(k + 1, 8):
            for j in range(r, 8):
                e[r, j] = e[r, j] - low[r, k] * e[k, j]
    full = [full[k] * inv[k] for k in range(8)]
    for k in range(7, 0, -1):
        for r in range(k):
            full[r] = full[r] - low[k, r] * full[k]
    top = full[0]
    for k in range(1, 8):
        top = jnp.where(sub == k, full[k], top)
    out = list(rows)
    out[p] = top
    for i, c in rest.items():
        t = [c[j] * full[j] for j in range(8)]
        s = ((t[0] + t[1]) + (t[2] + t[3])) + ((t[4] + t[5]) + (t[6] + t[7]))
        out[i] = jnp.where(inside, 0.0, rows[i]) - s
    return out


def inverse_128(a):
    lane = lax.broadcasted_iota(jnp.int32, (8, 128), 1)
    sub = lax.broadcasted_iota(jnp.int32, (8, 128), 0)

    def some(_, rows):
        for p in range(PER):
            rows = eliminate_eight(rows, p, lane, sub)
        rows = [pltpu.roll(v, 128 - 8 * PER, 1) for v in rows]
        return tuple(rows[PER:] + rows[:PER])

    rows = lax.fori_loop(0, 16 // PER, some, tuple(a[8 * i : 8 * i + 8, :] for i in range(16)))
    return jnp.concatenate(rows, axis=0)


def contract(a, b, dims):
    return lax.dot_general(a, b, (dims, ((), ())), precision=HI, preferred_element_type=F32)


def dot(a, b):
    return contract(a, b, ((1,), (0,)))


def dot_nt(a, b):
    return contract(a, b, ((1,), (1,)))


def dot_tn(a, b):
    return contract(a, b, ((0,), (0,)))


def inverse_in_place(ref):
    b = HALF // 2

    def step(i, _):
        at = pl.ds(pl.multiple_of(i * b, b), b)
        off = pl.ds(pl.multiple_of((1 - i) * b, b), b)
        pivot = inverse_128(ref[at, at])
        across = dot(pivot, ref[at, off])
        down = ref[off, at]
        ref[off, off] = ref[off, off] - dot(down, across)
        ref[off, at] = -dot(down, pivot)
        ref[at, off] = across
        ref[at, at] = pivot
        return 0

    lax.fori_loop(0, 2, step, 0)


def by_rows(n, body):
    def one(i, _):
        body(pl.ds(pl.multiple_of(i * 128, 128), 128))
        return 0

    lax.fori_loop(0, n // 128, one, 0)


def half_inverse(corner, below, inv_ref, low_ref, below_ref):
    inv_ref[...] = corner
    inverse_in_place(inv_ref)
    below_ref[...] = below

    def some(rows):
        low_ref[rows, :] = dot(below_ref[rows, :], inv_ref[...])

    by_rows(HALF, some)


def whole_inverse(corner, inv, low, below, out_ref, work):
    h = HALF
    work[...] = corner

    def schur(rows):
        work[rows, :] = work[rows, :] - dot_nt(low[rows, :], below[...])

    by_rows(h, schur)
    inverse_in_place(work)

    def lower(rows):
        out_ref[pl.ds(h + rows.start, 128), 0:h] = -dot(work[rows, :], low[...])

    by_rows(h, lower)

    def upper(rows):
        out_ref[rows, 0:h] = inv[rows, :] - dot_tn(low[:, rows], out_ref[h : 2 * h, 0:h])

    by_rows(h, upper)
    out_ref[h : 2 * h, h : 2 * h] = work[...]
    out_ref[0:h, h : 2 * h] = out_ref[h : 2 * h, 0:h].T


def half_one_kernel(mine, other, *outs):
    s = mine[...] + other[...]
    half_inverse(s[0:HALF], s[HALF : 2 * HALF], *outs)


def whole_one_kernel(mine, other, inv, low, below, out, work):
    whole_inverse(mine[...] + other[...], inv, low, below, out, work)


def half_two_kernel(where, mine, other, *outs):
    first = where[0] == 0
    half_inverse(
        jnp.where(first, mine[...], other[...]), jnp.where(first, other[...], mine[...]), *outs
    )


def whole_two_kernel(where, mine, other, inv, low, below, out, work):
    first = where[0] == 0
    corner = jnp.concatenate(
        [jnp.where(first, mine[...], other[...]), jnp.where(first, other[...], mine[...])], axis=0
    )
    whole_inverse(corner, inv, low, below, out, work)


SQUARE = jax.ShapeDtypeStruct((HALF, HALF), F32)
HALF_COST = 16 * 10**9


def pick_rows(idx_ref, start, src, dst, count):
    def eight(g, _):
        base = g * 8
        got = [src[pl.ds(idx_ref[start + base + i], 1), :] for i in range(8)]
        dst[pl.ds(pl.multiple_of(base, 8), 8), :] = jnp.concatenate(got, axis=0)
        return 0

    lax.fori_loop(0, count // 8, eight, 0)


def gather_kernel(idx_ref, a_ref, list_ref, *refs):
    parts, whole, rows = refs[:PARTS], refs[PARTS], refs[PARTS + 1]
    pick_rows(idx_ref, 0, a_ref, rows, EDGE)
    w = whole.shape[0]
    point = lax.broadcasted_iota(jnp.int32, (w, 1), 0) + lax.axis_index("col") * w
    hits = jnp.sum((list_ref[...] == point).astype(F32), axis=1, keepdims=True)
    keep = 1.0 - hits
    for k in range(0, EDGE, 128):
        t = rows[k : k + 128, :].T
        lo = k % HALF
        parts[k // HALF][:, lo : lo + 128] = t
        whole[:, k : k + 128] = t * keep


def select_kernel(start, count, idx_ref, *refs):
    pieces, o_ref, stack = refs[:COLS], refs[COLS], refs[COLS + 1]
    w = pieces[0].shape[0]
    for k, piece in enumerate(pieces):
        stack[k * w : (k + 1) * w, :] = piece[...]
    pick_rows(idx_ref, start, stack, o_ref, count)


def column_of(row, n):
    return jnp.broadcast_to(row, (128, n)).T


def half_of(parity):
    return pl.ds(pl.multiple_of(parity * HALF, HALF), HALF)


def middle_kernel(where, inv, t_own, t_sib, m_ref, mh_ref, ab_ref, d_ref, x_all, y_one):
    parity = where[0]
    x_all[:, half_of(parity)] = t_own[0:IFACE, :]
    x_all[:, half_of(1 - parity)] = t_sib[0:IFACE, :]
    y_one[...] = jnp.where(parity == 1, t_own[IFACE:EDGE, :], t_sib[IFACE:EDGE, :])

    def rows_of_m(rows):
        m_ref[rows, :] = dot(inv[rows, :], x_all[...])

    by_rows(IFACE, rows_of_m)
    mh_ref[...] = m_ref[half_of(parity), :]
    y_zero = jnp.where(parity == 0, t_own[IFACE:EDGE, :], 0.0)
    ab_ref[...] = y_zero

    def rows_of_ab(rows):
        ab_ref[rows, :] = ab_ref[rows, :] - dot_tn(t_own[0:IFACE, rows], m_ref[:, 0:HALF])

    by_rows(HALF, rows_of_ab)
    o = pl.multiple_of(parity * 128, 128)
    part = x_all[:, pl.ds(pl.multiple_of(HALF + parity * 128, 128), 128)]
    d_ref[...] = y_one[pl.ds(o, 128), :] - dot_tn(part, m_ref[:, HALF:IFACE])


def split(v):
    high = v.astype(BF16)
    return high, (v - high.astype(F32)).astype(BF16)


def three(a, b, dims=((1,), (0,))):
    def one(x, y):
        return lax.dot_general(x, y, (dims, ((), ())), preferred_element_type=F32)

    return one(a[0], b[0]) + (one(a[0], b[1]) + one(a[1], b[0]))


def side_kernel(where, inv, m, whole, gt_ref, w_ref):
    m2, inv2 = split(m[...]), split(inv[...])
    mine = half_of(where[0])

    def some(rows):
        pi = split(whole[rows, 0:IFACE])
        w_ref[rows, :] = three(pi, inv2)
        gt_ref[rows, :] = -three(pi, m2)
        gt_ref[rows, mine] = gt_ref[rows, mine] + whole[rows, IFACE:EDGE]

    by_rows(whole.shape[0], some)


def last_kernel(where, inv, m_ref, mz, mz_sib, gt, w1t, a_ref, keep2, keep_col, *refs):
    n_in = 2 * PARTS + 2 * (COLS + 1)
    ins, out = refs[:n_in], refs[n_in]
    edges, both, block, m_far, in_sems, out_sems = refs[n_in + 1 :]
    parity, quad, col = where[0], where[1], where[2]
    w = gt.shape[0]
    child = COLS * w
    copies = [[], [], [], []]

    def load(m, k, src, dst):
        c = pltpu.make_async_copy(src, dst, in_sems.at[m, k])
        c.start()
        copies[m].append(c)

    for m in range(2):
        for k in range(PARTS):
            dst = edges.at[pl.ds(m * child, child), pl.ds(k * HALF, HALF)]
            load(m, k, ins[PARTS * m + k], dst)
    for m in range(2):
        start = (2 + m) * child
        for k in range(COLS + 1):
            piece = ins[2 * PARTS + (COLS + 1) * m + k]
            load(2 + m, k, piece, edges.at[pl.ds(start, piece.shape[0]), :])
            start += piece.shape[0]

    m_far[half_of(parity), :] = mz[...]
    m_far[half_of(1 - parity), :] = mz_sib[...]
    nt = ((1,), (1,))
    inv2, near2, far2 = split(inv[...]), split(m_ref[...]), split(m_far[...])

    def some(rows):
        vt = three(split(gt[rows, :]), inv2)
        vt2 = split(vt)
        u = split((w1t[rows, :] - three(vt2, near2, nt)).T)
        f = split((-three(vt2, far2, nt)).T)
        v = split(vt.T)
        for part in range(2):
            lanes = pl.ds(pl.multiple_of(part * w + rows.start, 128), 128)
            for k in range(4):
                both[k, 0:IFACE, lanes] = (u if k < 2 else f)[part]
            for k in range(2):
                half = v[part][k * HALF : (k + 1) * HALF]
                same = k ^ parity
                both[same, IFACE:EDGE, lanes] = half
                both[same + 2, IFACE:EDGE, lanes] = half

    by_rows(w, some)

    def store(i):
        m, r = i // COLS, i % COLS
        o = (quad ^ m) * child + ((col + r) % COLS) * w
        return pltpu.make_async_copy(
            block.at[i % 2], out.at[pl.ds(pl.multiple_of(o, w), w), :], out_sems.at[i % 2]
        )

    def one(i, _):
        m, r = i // COLS, i % COLS
        for k in range(4):

            @pl.when(i == k * COLS)
            def _():
                for c in copies[k]:
                    c.wait()

        @pl.when(i >= 2)
        def _():
            store(i - 2).wait()

        high, low = split(edges[pl.ds(pl.multiple_of(i * w, w), w), :])
        wide = jnp.dot(high, both[m], preferred_element_type=F32)
        total = wide[:, 0:w] + (
            wide[:, w : 2 * w] + jnp.dot(low, both[m, :, 0:w], preferred_element_type=F32)
        )
        block[i % 2] = -total

        @pl.when(m < 2)
        def _():
            here = pl.ds(pl.multiple_of(((col + r) % COLS) * w, w), w)
            mask = jnp.tile(column_of(keep2[pl.ds(jnp.minimum(m, 1), 1), here], w), (1, w // 128))
            own = jnp.where(m == 0, keep_col[...], 0.0)
            block[i % 2] = (block[i % 2] + a_ref[here, :] * own) * mask

        store(i).start()
        return 0

    lax.fori_loop(0, 4 * COLS, one, 0)
    store(4 * COLS - 2).wait()
    store(4 * COLS - 1).wait()


def swapped(shard, apart):
    n = lax.axis_size("box")
    return lax.ppermute(shard, "box", [(i, i ^ apart) for i in range(n)])


def shifted(shard, by):
    return lax.ppermute(shard, "col", [((i + by) % COLS, i) for i in range(COLS)])


def after(values, *others):
    return lax.optimization_barrier((values, others))[0]


def around(own, forward):
    right, left = shifted(own, 1), shifted(own, -1)
    return (own, right, left), (right if forward == 1 else left)


def farther(near, forward):
    own, right, left = near
    far = shifted(right if forward == 1 else left, forward)
    return own, right, far, left


def farther_both(near, done):
    own, right, left = near
    h = own.shape[0] // 2
    top, bottom = after((right[:h], left[h:]), done)
    far = shifted(top, 1), shifted(bottom, -1)
    return own, right, *far, left


def select(start, count, relative, pieces):
    rows = COLS * pieces[0].shape[0]
    return call(
        functools.partial(select_kernel, start, count),
        (shape(count, HALF), shape(rows, HALF)),
        1,
        COLS,
        3 * 10**9,
        8 * rows * HALF,
    )(relative, *pieces)


def merged(child_maps, iface_one, iface_two):
    a = child_maps[0]
    boundary, w = a.shape
    box, col = lax.axis_index("box"), lax.axis_index("col")
    parity = box % 2
    own_one = iface_one[0]
    group = lax.dynamic_index_in_dim(iface_two, box // 2, 0, keepdims=False)
    own_two = lax.dynamic_slice_in_dim(group, parity * HALF, HALF) - parity * boundary
    points = jnp.concatenate([own_one, own_two])

    *parts, whole = call(
        gather_kernel,
        (shape(w, HALF),) * PARTS + (shape(w, EDGE),),
        1,
        2,
        0,
        4 * boundary * w,
        [pltpu.VMEM((EDGE, w), F32)],
    )(points, a, points[None, :])
    near0, first0 = around(parts[0], 1)
    part0 = farther(near0, 1)
    relative = (points - col * w) % boundary
    where = jnp.stack([parity, box % 4, col]).astype(jnp.int32)
    near1, first1 = around(after(parts[1], first0), -1)
    part1 = farther(near1, -1)
    far = swapped(whole, 2)
    matches = jnp.arange(boundary, dtype=jnp.int32)[None, :] == points[:, None]
    keep = 1.0 - jnp.sum(matches.astype(F32), axis=0)
    keep_col = lax.dynamic_slice_in_dim(keep, col * w, w)[None, :]
    keep2 = jnp.stack([keep, swapped(keep, 1)])

    t0, stack0 = select(0, IFACE, relative, part0)
    t0, t0_sib, where, keep2, keep_col = after(
        (t0, swapped(t0, 1), where, keep2, keep_col), first1
    )
    half = call(half_one_kernel, (SQUARE,) * 3, 0, 2, HALF_COST, 10**6)(t0, t0_sib)

    near2, first2 = around(after(parts[2], first1), 1)
    far2 = shifted(after(parts[2], first1), 2)
    part2 = near2[0], near2[1], far2, near2[2]
    t1, stack1 = select(HALF, HALF, relative, after(part1, half[0]))
    t1, t1_sib = after((t1, swapped(t1, 1)), first2)
    inv_one = call(
        whole_one_kernel, shape(IFACE, IFACE), 0, 5, HALF_COST, 10**6,
        [pltpu.VMEM((HALF, HALF), F32)],
    )(t1, t1_sib, *half)

    nearz, _ = around(after(far, first2), -1)
    t2, stack2 = select(0, EDGE, relative, after(part2, inv_one))
    m, m_half, ab, d = call(
        middle_kernel,
        (shape(IFACE, IFACE), shape(HALF, IFACE), SQUARE, shape(128, HALF)),
        1,
        3,
        5 * 10**9,
        2**22,
        [pltpu.VMEM((IFACE, IFACE), F32), pltpu.VMEM((HALF, HALF), F32)],
    )(where, inv_one, t2, swapped(t2, 1))

    ab_far = swapped(ab, 2)
    gt, w1t = call(
        side_kernel, (shape(w, IFACE),) * 2, 1, 3, 3 * 10**9, 2**22
    )(where, inv_one, m, whole)
    partz = farther_both(nearz, gt)
    ab = ab + after(ab_far, gt)
    ab_sib = swapped(ab, 1)
    d = after(d, ab_far)
    d = d + swapped(d, 2)
    d_sib = swapped(d, 1)
    half = call(half_two_kernel, (SQUARE,) * 3, 1, 2, HALF_COST, 10**6)(where, ab, ab_sib)
    inv_two = call(
        whole_two_kernel, shape(IFACE, IFACE), 1, 5, HALF_COST, 10**6,
        [pltpu.VMEM((HALF, HALF), F32)],
    )(where, d, d_sib, *half)

    m_far = swapped(after(m_half, d), 2)
    stacks = (stack0, stack1, stack2)
    stacks_sib = [swapped(v, 1) for v in stacks]
    partz_sib = [swapped(v, 1) for v in partz]
    out = pl.pallas_call(
        last_kernel,
        name="last",
        out_shape=shape(COLS * boundary, w),
        in_specs=[SMEM] + [VMEM] * 9 + [ANY] * (2 * PARTS + 2 * (COLS + 1)),
        out_specs=ANY,
        scratch_shapes=[
            pltpu.VMEM((4 * boundary, EDGE), F32),
            pltpu.VMEM((4, EDGE, 2 * w), BF16),
            pltpu.VMEM((2, w, w), F32),
            pltpu.VMEM((IFACE, IFACE), F32),
            pltpu.SemaphoreType.DMA((4, COLS + 1)),
            pltpu.SemaphoreType.DMA((2,)),
        ],
        cost_estimate=pl.CostEstimate(flops=10**10, bytes_accessed=3 * 10**7, transcendentals=0),
        compiler_params=pltpu.CompilerParams(vmem_limit_bytes=48 * 2**20),
    )(
        where, inv_two, m, m_far, swapped(m_far, 1), gt, w1t, a, keep2, keep_col,
        *stacks, *stacks_sib, *partz, *partz_sib,
    )
    return out[None]


def solution(mesh):
    return jax.shard_map(
        merged,
        mesh=mesh,
        in_specs=(P("box", None, "col"), P("box", None), P()),
        out_specs=P("box", None, "col"),
        check_vma=False,
    )
```

```python
import functools

import jax
import jax.numpy as jnp
from jax import lax
from jax.experimental import pallas as pl
from jax.experimental.pallas import tpu as pltpu
from jax.sharding import PartitionSpec as P

F32 = jnp.float32
BF16 = jnp.bfloat16
HI = lax.Precision.HIGHEST
COLS = 4
IFACE = 512
HALF = 256
EDGE = IFACE + HALF
PARTS = EDGE // HALF


TOGETHER = 2
PER = 4

VMEM = pl.BlockSpec(memory_space=pltpu.VMEM)
SMEM = pl.BlockSpec(memory_space=pltpu.SMEM)
ANY = pl.BlockSpec(memory_space=pl.ANY)


def call(body, outs, n_smem, n_in, flops, nbytes, scratch=()):
    return pl.pallas_call(
        body,
        out_shape=outs,
        in_specs=[SMEM] * n_smem + [VMEM] * n_in,
        out_specs=jax.tree.map(lambda _: VMEM, outs),
        scratch_shapes=scratch,
        cost_estimate=pl.CostEstimate(flops=flops, bytes_accessed=nbytes, transcendentals=0),
        compiler_params=pltpu.CompilerParams(vmem_limit_bytes=20 * 2**20),
    )


def shape(*dims):
    return jax.ShapeDtypeStruct(dims, F32)


def lane_of(v, j):
    return jnp.broadcast_to(v[:, j : j + 1], v.shape)


def row_of(v, r):
    return jnp.broadcast_to(v[r : r + 1, :], v.shape)


def eliminate_eight(rows, p, lane, sub):
    off = 8 * p
    full = [row_of(rows[p], k) for k in range(8)]
    e = {(k, j): lane_of(full[k], off + j) for k in range(8) for j in range(k, 8)}
    rest = {i: [lane_of(rows[i], off + j) for j in range(8)] for i in range(16) if i != p}
    inside = (lane >= off) & (lane < off + 8)
    full = [jnp.where(inside, jnp.where(lane == off + k, 1.0, 0.0), full[k]) for k in range(8)]
    low, inv = {}, []
    for k in range(8):
        inv.append(1.0 / e[k, k])
        for r in range(k + 1, 8):
            low[r, k] = e[k, r] * inv[k]
            full[r] = full[r] - low[r, k] * full[k]
        for r in range(k + 1, 8):
            for j in range(r, 8):
                e[r, j] = e[r, j] - low[r, k] * e[k, j]
    full = [full[k] * inv[k] for k in range(8)]
    for k in range(7, 0, -1):
        for r in range(k):
            full[r] = full[r] - low[k, r] * full[k]
    top = full[0]
    for k in range(1, 8):
        top = jnp.where(sub == k, full[k], top)
    out = list(rows)
    out[p] = top
    for i, c in rest.items():
        t = [c[j] * full[j] for j in range(8)]
        s = ((t[0] + t[1]) + (t[2] + t[3])) + ((t[4] + t[5]) + (t[6] + t[7]))
        out[i] = jnp.where(inside, 0.0, rows[i]) - s
    return out


def inverse_128(a):
    lane = lax.broadcasted_iota(jnp.int32, (8, 128), 1)
    sub = lax.broadcasted_iota(jnp.int32, (8, 128), 0)

    def some(_, rows):
        for p in range(PER):
            rows = eliminate_eight(rows, p, lane, sub)
        rows = [pltpu.roll(v, 128 - 8 * PER, 1) for v in rows]
        return tuple(rows[PER:] + rows[:PER])

    rows = lax.fori_loop(0, 16 // PER, some, tuple(a[8 * i : 8 * i + 8, :] for i in range(16)))
    return jnp.concatenate(rows, axis=0)


def contract(a, b, dims):
    return lax.dot_general(a, b, (dims, ((), ())), precision=HI, preferred_element_type=F32)


def dot(a, b):
    return contract(a, b, ((1,), (0,)))


def dot_nt(a, b):
    return contract(a, b, ((1,), (1,)))


def dot_tn(a, b):
    return contract(a, b, ((0,), (0,)))


def inverse_in_place(ref):
    b = HALF // 2

    def step(i, _):
        at = pl.ds(pl.multiple_of(i * b, b), b)
        off = pl.ds(pl.multiple_of((1 - i) * b, b), b)
        pivot = inverse_128(ref[at, at])
        across = dot(pivot, ref[at, off])
        down = ref[off, at]
        ref[off, off] = ref[off, off] - dot(down, across)
        ref[off, at] = -dot(down, pivot)
        ref[at, off] = across
        ref[at, at] = pivot
        return 0

    lax.fori_loop(0, 2, step, 0)


def by_rows(n, body):
    def one(i, _):
        body(pl.ds(pl.multiple_of(i * 128, 128), 128))
        return 0

    lax.fori_loop(0, n // 128, one, 0)


def half_inverse(corner, below, inv_ref, low_ref, below_ref):
    inv_ref[...] = corner
    inverse_in_place(inv_ref)
    below_ref[...] = below

    def some(rows):
        low_ref[rows, :] = dot(below_ref[rows, :], inv_ref[...])

    by_rows(HALF, some)


def whole_inverse(corner, inv, low, below, out_ref, work):
    h = HALF
    work[...] = corner

    def schur(rows):
        work[rows, :] = work[rows, :] - dot_nt(low[rows, :], below[...])

    by_rows(h, schur)
    inverse_in_place(work)

    def lower(rows):
        out_ref[pl.ds(h + rows.start, 128), 0:h] = -dot(work[rows, :], low[...])

    by_rows(h, lower)

    def upper(rows):
        out_ref[rows, 0:h] = inv[rows, :] - dot_tn(low[:, rows], out_ref[h : 2 * h, 0:h])

    by_rows(h, upper)
    out_ref[h : 2 * h, h : 2 * h] = work[...]
    out_ref[0:h, h : 2 * h] = out_ref[h : 2 * h, 0:h].T


def half_one_kernel(mine, other, *outs):
    s = mine[...] + other[...]
    half_inverse(s[0:HALF], s[HALF : 2 * HALF], *outs)


def whole_one_kernel(mine, other, inv, low, below, out, work):
    whole_inverse(mine[...] + other[...], inv, low, below, out, work)


def half_two_kernel(where, mine, other, *outs):
    first = where[0] == 0
    half_inverse(
        jnp.where(first, mine[...], other[...]), jnp.where(first, other[...], mine[...]), *outs
    )


def whole_two_kernel(where, mine, other, inv, low, below, out, work):
    first = where[0] == 0
    corner = jnp.concatenate(
        [jnp.where(first, mine[...], other[...]), jnp.where(first, other[...], mine[...])], axis=0
    )
    whole_inverse(corner, inv, low, below, out, work)


SQUARE = jax.ShapeDtypeStruct((HALF, HALF), F32)
HALF_COST = 16 * 10**9


def pick_rows(idx_ref, start, src, dst, count):
    def eight(g, _):
        base = g * 8
        got = [src[pl.ds(idx_ref[start + base + i], 1), :] for i in range(8)]
        dst[pl.ds(pl.multiple_of(base, 8), 8), :] = jnp.concatenate(got, axis=0)
        return 0

    lax.fori_loop(0, count // 8, eight, 0)


def gather_kernel(idx_ref, a_ref, list_ref, *refs):
    parts, whole, rows = refs[:PARTS], refs[PARTS], refs[PARTS + 1]
    pick_rows(idx_ref, 0, a_ref, rows, EDGE)
    w = whole.shape[0]
    point = lax.broadcasted_iota(jnp.int32, (w, 1), 0) + lax.axis_index("col") * w
    hits = jnp.sum((list_ref[...] == point).astype(F32), axis=1, keepdims=True)
    keep = 1.0 - hits
    for k in range(0, EDGE, 128):
        t = rows[k : k + 128, :].T
        lo = k % HALF
        parts[k // HALF][:, lo : lo + 128] = t
        whole[:, k : k + 128] = t * keep


def select_kernel(start, count, idx_ref, *refs):
    pieces, o_ref, stack = refs[:COLS], refs[COLS], refs[COLS + 1]
    w = pieces[0].shape[0]
    for k, piece in enumerate(pieces):
        stack[k * w : (k + 1) * w, :] = piece[...]
    pick_rows(idx_ref, start, stack, o_ref, count)


def column_of(row, n):
    return jnp.broadcast_to(row, (128, n)).T


def half_of(parity):
    return pl.ds(pl.multiple_of(parity * HALF, HALF), HALF)


def middle_kernel(where, inv, t_own, t_sib, m_ref, mh_ref, ab_ref, d_ref, x_all, y_one):
    parity = where[0]
    x_all[:, half_of(parity)] = t_own[0:IFACE, :]
    x_all[:, half_of(1 - parity)] = t_sib[0:IFACE, :]
    y_one[...] = jnp.where(parity == 1, t_own[IFACE:EDGE, :], t_sib[IFACE:EDGE, :])

    def rows_of_m(rows):
        m_ref[rows, :] = dot(inv[rows, :], x_all[...])

    by_rows(IFACE, rows_of_m)
    mh_ref[...] = m_ref[half_of(parity), :]
    y_zero = jnp.where(parity == 0, t_own[IFACE:EDGE, :], 0.0)
    ab_ref[...] = y_zero

    def rows_of_ab(rows):
        ab_ref[rows, :] = ab_ref[rows, :] - dot_tn(t_own[0:IFACE, rows], m_ref[:, 0:HALF])

    by_rows(HALF, rows_of_ab)
    o = pl.multiple_of(parity * 128, 128)
    part = x_all[:, pl.ds(pl.multiple_of(HALF + parity * 128, 128), 128)]
    d_ref[...] = y_one[pl.ds(o, 128), :] - dot_tn(part, m_ref[:, HALF:IFACE])


def split(v):
    high = v.astype(BF16)
    return high, (v - high.astype(F32)).astype(BF16)


def three(a, b, dims=((1,), (0,))):
    def one(x, y):
        return lax.dot_general(x, y, (dims, ((), ())), preferred_element_type=F32)

    return one(a[0], b[0]) + (one(a[0], b[1]) + one(a[1], b[0]))


def side_kernel(where, inv, m, whole, gt_ref, w_ref):
    m2, inv2 = split(m[...]), split(inv[...])
    mine = half_of(where[0])

    def some(rows):
        pi = split(whole[rows, 0:IFACE])
        w_ref[rows, :] = three(pi, inv2)
        gt_ref[rows, :] = -three(pi, m2)
        gt_ref[rows, mine] = gt_ref[rows, mine] + whole[rows, IFACE:EDGE]

    by_rows(whole.shape[0], some)


def last_kernel(where, inv, m_ref, mz, mz_sib, gt, w1t, a_ref, keep2, keep_col, *refs):
    n_in = 2 * PARTS + 2 * (COLS + 1)
    ins, out = refs[:n_in], refs[n_in]
    edges, both, block, m_far, in_sems, out_sems = refs[n_in + 1 :]
    parity, quad, col = where[0], where[1], where[2]
    w = gt.shape[0]
    child = COLS * w
    copies = [[], [], [], []]

    def load(m, k, src, dst):
        c = pltpu.make_async_copy(src, dst, in_sems.at[m, k])
        c.start()
        copies[m].append(c)

    for m in range(2):
        for k in range(PARTS):
            dst = edges.at[pl.ds(m * child, child), pl.ds(k * HALF, HALF)]
            load(m, k, ins[PARTS * m + k], dst)
    for m in range(2):
        start = (2 + m) * child
        for k in range(COLS + 1):
            piece = ins[2 * PARTS + (COLS + 1) * m + k]
            load(2 + m, k, piece, edges.at[pl.ds(start, piece.shape[0]), :])
            start += piece.shape[0]

    m_far[half_of(parity), :] = mz[...]
    m_far[half_of(1 - parity), :] = mz_sib[...]
    nt = ((1,), (1,))
    inv2, near2, far2 = split(inv[...]), split(m_ref[...]), split(m_far[...])

    def some(rows):
        vt = three(split(gt[rows, :]), inv2)
        vt2 = split(vt)
        u = split((w1t[rows, :] - three(vt2, near2, nt)).T)
        f = split((-three(vt2, far2, nt)).T)
        v = split(vt.T)
        for part in range(2):
            lanes = pl.ds(pl.multiple_of(part * w + rows.start, 128), 128)
            for k in range(4):
                both[k, 0:IFACE, lanes] = (u if k < 2 else f)[part]
            for k in range(2):
                half = v[part][k * HALF : (k + 1) * HALF]
                same = k ^ parity
                both[same, IFACE:EDGE, lanes] = half
                both[same + 2, IFACE:EDGE, lanes] = half

    by_rows(w, some)

    def store(i, j):
        m, r = i * TOGETHER // COLS, i * TOGETHER % COLS + j
        o = (quad ^ m) * child + ((col + r) % COLS) * w
        return pltpu.make_async_copy(
            block.at[i % 2, pl.ds(j * w, w), :],
            out.at[pl.ds(pl.multiple_of(o, w), w), :],
            out_sems.at[i % 2, j],
        )

    def one(i, _):
        m, r = i * TOGETHER // COLS, i * TOGETHER % COLS
        for k in range(4):

            @pl.when(i == k * COLS // TOGETHER)
            def _():
                for c in copies[k]:
                    c.wait()

        @pl.when(i >= 2)
        def _():
            for j in range(TOGETHER):
                store(i - 2, j).wait()

        size = TOGETHER * w
        high, low = split(edges[pl.ds(pl.multiple_of(i * size, size), size), :])
        wide = jnp.dot(high, both[m], preferred_element_type=F32)
        total = wide[:, 0:w] + (
            wide[:, w : 2 * w] + jnp.dot(low, both[m, :, 0:w], preferred_element_type=F32)
        )
        block[i % 2] = -total

        @pl.when(m < 2)
        def _():
            own = jnp.where(m == 0, keep_col[...], 0.0)
            for j in range(TOGETHER):
                here = pl.ds(pl.multiple_of(((col + r + j) % COLS) * w, w), w)
                rows = slice(j * w, (j + 1) * w)
                mask = column_of(keep2[pl.ds(jnp.minimum(m, 1), 1), here], w)
                block[i % 2, rows] = (block[i % 2, rows] + a_ref[here, :] * own) * jnp.tile(
                    mask, (1, w // 128)
                )

        for j in range(TOGETHER):
            store(i, j).start()
        return 0

    steps = 4 * COLS // TOGETHER
    lax.fori_loop(0, steps, one, 0)
    for j in range(TOGETHER):
        store(steps - 2, j).wait()
        store(steps - 1, j).wait()


def swapped(shard, apart):
    n = lax.axis_size("box")
    return lax.ppermute(shard, "box", [(i, i ^ apart) for i in range(n)])


def shifted(shard, by):
    return lax.ppermute(shard, "col", [((i + by) % COLS, i) for i in range(COLS)])


def after(values, *others):
    return lax.optimization_barrier((values, others))[0]


def around(own, forward):
    right, left = shifted(own, 1), shifted(own, -1)
    return (own, right, left), (right if forward == 1 else left)


def farther(near, forward):
    own, right, left = near
    far = shifted(right if forward == 1 else left, forward)
    return own, right, far, left


def farther_both(near, done):
    own, right, left = near
    h = own.shape[0] // 2
    top, bottom = after((right[:h], left[h:]), done)
    far = shifted(top, 1), shifted(bottom, -1)
    return own, right, *far, left


def select(start, count, relative, pieces):
    rows = COLS * pieces[0].shape[0]
    return call(
        functools.partial(select_kernel, start, count),
        (shape(count, HALF), shape(rows, HALF)),
        1,
        COLS,
        3 * 10**9,
        8 * rows * HALF,
    )(relative, *pieces)


def merged(child_maps, iface_one, iface_two):
    a = child_maps[0]
    boundary, w = a.shape
    box, col = lax.axis_index("box"), lax.axis_index("col")
    parity = box % 2
    own_one = iface_one[0]
    group = lax.dynamic_index_in_dim(iface_two, box // 2, 0, keepdims=False)
    own_two = lax.dynamic_slice_in_dim(group, parity * HALF, HALF) - parity * boundary
    points = jnp.concatenate([own_one, own_two])

    *parts, whole = call(
        gather_kernel,
        (shape(w, HALF),) * PARTS + (shape(w, EDGE),),
        1,
        2,
        0,
        4 * boundary * w,
        [pltpu.VMEM((EDGE, w), F32)],
    )(points, a, points[None, :])
    near0, first0 = around(parts[0], 1)
    part0 = farther(near0, 1)
    relative = (points - col * w) % boundary
    where = jnp.stack([parity, box % 4, col]).astype(jnp.int32)
    near1, first1 = around(after(parts[1], first0), -1)
    part1 = farther(near1, -1)
    far = swapped(whole, 2)
    matches = jnp.arange(boundary, dtype=jnp.int32)[None, :] == points[:, None]
    keep = 1.0 - jnp.sum(matches.astype(F32), axis=0)
    keep_col = lax.dynamic_slice_in_dim(keep, col * w, w)[None, :]
    keep2 = jnp.stack([keep, swapped(keep, 1)])

    t0, stack0 = select(0, IFACE, relative, part0)
    t0, t0_sib, where, keep2, keep_col = after(
        (t0, swapped(t0, 1), where, keep2, keep_col), first1
    )
    half = call(half_one_kernel, (SQUARE,) * 3, 0, 2, HALF_COST, 10**6)(t0, t0_sib)

    right2 = shifted(after(parts[2], first0), 1)
    own2 = after(parts[2], first1)
    left2, far2 = shifted(own2, -1), shifted(own2, 2)
    part2, first2 = (parts[2], right2, far2, left2), right2
    t1, stack1 = select(HALF, HALF, relative, after(part1, half[0]))
    t1, t1_sib = after((t1, swapped(t1, 1)), first2)
    inv_one = call(
        whole_one_kernel, shape(IFACE, IFACE), 0, 5, HALF_COST, 10**6,
        [pltpu.VMEM((HALF, HALF), F32)],
    )(t1, t1_sib, *half)

    nearz, _ = around(after(far, first2), -1)
    t2, stack2 = select(0, EDGE, relative, after(part2, inv_one))
    m, m_half, ab, d = call(
        middle_kernel,
        (shape(IFACE, IFACE), shape(HALF, IFACE), SQUARE, shape(128, HALF)),
        1,
        3,
        5 * 10**9,
        2**22,
        [pltpu.VMEM((IFACE, IFACE), F32), pltpu.VMEM((HALF, HALF), F32)],
    )(where, inv_one, t2, swapped(t2, 1))

    ab_far = swapped(ab, 2)
    gt, w1t = call(
        side_kernel, (shape(w, IFACE),) * 2, 1, 3, 3 * 10**9, 2**22
    )(where, inv_one, m, whole)
    partz = farther_both(nearz, gt)
    ab = ab + after(ab_far, gt)
    ab_sib = swapped(ab, 1)
    d = after(d, ab_far)
    d = d + swapped(d, 2)
    d_sib = swapped(d, 1)
    half = call(half_two_kernel, (SQUARE,) * 3, 1, 2, HALF_COST, 10**6)(where, ab, ab_sib)
    inv_two = call(
        whole_two_kernel, shape(IFACE, IFACE), 1, 5, HALF_COST, 10**6,
        [pltpu.VMEM((HALF, HALF), F32)],
    )(where, d, d_sib, *half)

    m_far = swapped(after(m_half, d), 2)
    stacks = (stack0, stack1, stack2)
    stacks_sib = [swapped(v, 1) for v in stacks]
    partz_sib = [swapped(v, 1) for v in partz]
    out = pl.pallas_call(
        last_kernel,
        name="last",
        out_shape=shape(COLS * boundary, w),
        in_specs=[SMEM] + [VMEM] * 9 + [ANY] * (2 * PARTS + 2 * (COLS + 1)),
        out_specs=ANY,
        scratch_shapes=[
            pltpu.VMEM((4 * boundary, EDGE), F32),
            pltpu.VMEM((4, EDGE, 2 * w), BF16),
            pltpu.VMEM((2, TOGETHER * w, w), F32),
            pltpu.VMEM((IFACE, IFACE), F32),
            pltpu.SemaphoreType.DMA((4, COLS + 1)),
            pltpu.SemaphoreType.DMA((2, TOGETHER)),
        ],
        cost_estimate=pl.CostEstimate(flops=10**10, bytes_accessed=3 * 10**7, transcendentals=0),
        compiler_params=pltpu.CompilerParams(vmem_limit_bytes=48 * 2**20),
    )(
        where, inv_two, m, m_far, swapped(m_far, 1), gt, w1t, a, keep2, keep_col,
        *stacks, *stacks_sib, *partz, *partz_sib,
    )
    return out[None]


def solution(mesh):
    return jax.shard_map(
        merged,
        mesh=mesh,
        in_specs=(P("box", None, "col"), P("box", None), P()),
        out_specs=P("box", None, "col"),
        check_vma=False,
    )
```

```python
import functools

import jax
import jax.numpy as jnp
from jax import lax
from jax.experimental import pallas as pl
from jax.experimental.pallas import tpu as pltpu
from jax.sharding import PartitionSpec as P

F32 = jnp.float32
BF16 = jnp.bfloat16
HI = lax.Precision.HIGHEST
COLS = 4
IFACE = 512
HALF = 256
EDGE = IFACE + HALF
PARTS = EDGE // HALF


TOGETHER = 2
PER = 4

VMEM = pl.BlockSpec(memory_space=pltpu.VMEM)
SMEM = pl.BlockSpec(memory_space=pltpu.SMEM)
ANY = pl.BlockSpec(memory_space=pl.ANY)


def call(body, outs, n_smem, n_in, flops, nbytes, scratch=()):
    return pl.pallas_call(
        body,
        out_shape=outs,
        in_specs=[SMEM] * n_smem + [VMEM] * n_in,
        out_specs=jax.tree.map(lambda _: VMEM, outs),
        scratch_shapes=scratch,
        cost_estimate=pl.CostEstimate(flops=flops, bytes_accessed=nbytes, transcendentals=0),
        compiler_params=pltpu.CompilerParams(vmem_limit_bytes=20 * 2**20),
    )


def shape(*dims):
    return jax.ShapeDtypeStruct(dims, F32)


def lane_of(v, j):
    return jnp.broadcast_to(v[:, j : j + 1], v.shape)


def row_of(v, r):
    return jnp.broadcast_to(v[r : r + 1, :], v.shape)


def eliminate_eight(rows, p, lane, sub):
    off = 8 * p
    full = [row_of(rows[p], k) for k in range(8)]
    e = {(k, j): lane_of(full[k], off + j) for k in range(8) for j in range(k, 8)}
    rest = {i: [lane_of(rows[i], off + j) for j in range(8)] for i in range(16) if i != p}
    inside = (lane >= off) & (lane < off + 8)
    full = [jnp.where(inside, jnp.where(lane == off + k, 1.0, 0.0), full[k]) for k in range(8)]
    low, inv = {}, []
    for k in range(8):
        inv.append(1.0 / e[k, k])
        for r in range(k + 1, 8):
            low[r, k] = e[k, r] * inv[k]
            full[r] = full[r] - low[r, k] * full[k]
        for r in range(k + 1, 8):
            for j in range(r, 8):
                e[r, j] = e[r, j] - low[r, k] * e[k, j]
    full = [full[k] * inv[k] for k in range(8)]
    for k in range(7, 0, -1):
        for r in range(k):
            full[r] = full[r] - low[k, r] * full[k]
    top = full[0]
    for k in range(1, 8):
        top = jnp.where(sub == k, full[k], top)
    out = list(rows)
    out[p] = top
    for i, c in rest.items():
        t = [c[j] * full[j] for j in range(8)]
        s = ((t[0] + t[1]) + (t[2] + t[3])) + ((t[4] + t[5]) + (t[6] + t[7]))
        out[i] = jnp.where(inside, 0.0, rows[i]) - s
    return out


def inverse_128(a):
    lane = lax.broadcasted_iota(jnp.int32, (8, 128), 1)
    sub = lax.broadcasted_iota(jnp.int32, (8, 128), 0)

    def some(_, rows):
        for p in range(PER):
            rows = eliminate_eight(rows, p, lane, sub)
        rows = [pltpu.roll(v, 128 - 8 * PER, 1) for v in rows]
        return tuple(rows[PER:] + rows[:PER])

    rows = lax.fori_loop(0, 16 // PER, some, tuple(a[8 * i : 8 * i + 8, :] for i in range(16)))
    return jnp.concatenate(rows, axis=0)


def contract(a, b, dims):
    return lax.dot_general(a, b, (dims, ((), ())), precision=HI, preferred_element_type=F32)


def dot(a, b):
    return contract(a, b, ((1,), (0,)))


def dot_nt(a, b):
    return contract(a, b, ((1,), (1,)))


def dot_tn(a, b):
    return contract(a, b, ((0,), (0,)))


def inverse_in_place(ref):
    b = HALF // 2

    def step(i, _):
        at = pl.ds(pl.multiple_of(i * b, b), b)
        off = pl.ds(pl.multiple_of((1 - i) * b, b), b)
        pivot = inverse_128(ref[at, at])
        across = dot(pivot, ref[at, off])
        down = ref[off, at]
        ref[off, off] = ref[off, off] - dot(down, across)
        ref[off, at] = -dot(down, pivot)
        ref[at, off] = across
        ref[at, at] = pivot
        return 0

    lax.fori_loop(0, 2, step, 0)


def by_rows(n, body):
    def one(i, _):
        body(pl.ds(pl.multiple_of(i * 128, 128), 128))
        return 0

    lax.fori_loop(0, n // 128, one, 0)


def half_inverse(corner, below, inv_ref, low_ref, below_ref):
    inv_ref[...] = corner
    inverse_in_place(inv_ref)
    below_ref[...] = below

    def some(rows):
        low_ref[rows, :] = dot(below_ref[rows, :], inv_ref[...])

    by_rows(HALF, some)


def whole_inverse(corner, inv, low, below, out_ref, work):
    h = HALF
    work[...] = corner

    def schur(rows):
        work[rows, :] = work[rows, :] - dot_nt(low[rows, :], below[...])

    by_rows(h, schur)
    inverse_in_place(work)

    def lower(rows):
        out_ref[pl.ds(h + rows.start, 128), 0:h] = -dot(work[rows, :], low[...])

    by_rows(h, lower)

    def upper(rows):
        out_ref[rows, 0:h] = inv[rows, :] - dot_tn(low[:, rows], out_ref[h : 2 * h, 0:h])

    by_rows(h, upper)
    out_ref[h : 2 * h, h : 2 * h] = work[...]
    out_ref[0:h, h : 2 * h] = out_ref[h : 2 * h, 0:h].T


def half_one_kernel(mine, other, *outs):
    s = mine[...] + other[...]
    half_inverse(s[0:HALF], s[HALF : 2 * HALF], *outs)


def whole_one_kernel(mine, other, inv, low, below, out, work):
    whole_inverse(mine[...] + other[...], inv, low, below, out, work)


def half_two_kernel(where, mine, other, *outs):
    first = where[0] == 0
    half_inverse(
        jnp.where(first, mine[...], other[...]), jnp.where(first, other[...], mine[...]), *outs
    )


def whole_two_kernel(where, mine, other, inv, low, below, out, work):
    first = where[0] == 0
    corner = jnp.concatenate(
        [jnp.where(first, mine[...], other[...]), jnp.where(first, other[...], mine[...])], axis=0
    )
    whole_inverse(corner, inv, low, below, out, work)


SQUARE = jax.ShapeDtypeStruct((HALF, HALF), F32)
HALF_COST = 16 * 10**9


def pick_rows(idx_ref, start, src, dst, count):
    def eight(g, _):
        base = g * 8
        got = [src[pl.ds(idx_ref[start + base + i], 1), :] for i in range(8)]
        dst[pl.ds(pl.multiple_of(base, 8), 8), :] = jnp.concatenate(got, axis=0)
        return 0

    lax.fori_loop(0, count // 8, eight, 0)


def gather_kernel(idx_ref, a_ref, list_ref, *refs):
    parts, whole, rows = refs[:PARTS], refs[PARTS], refs[PARTS + 1]
    pick_rows(idx_ref, 0, a_ref, rows, EDGE)
    w = whole.shape[0]
    point = lax.broadcasted_iota(jnp.int32, (w, 1), 0) + lax.axis_index("col") * w
    hits = jnp.sum((list_ref[...] == point).astype(F32), axis=1, keepdims=True)
    keep = 1.0 - hits
    for k in range(0, EDGE, 128):
        t = rows[k : k + 128, :].T
        lo = k % HALF
        parts[k // HALF][:, lo : lo + 128] = t
        whole[:, k : k + 128] = t * keep


def select_kernel(start, count, idx_ref, *refs):
    pieces, o_ref, stack = refs[:COLS], refs[COLS], refs[COLS + 1]
    w = pieces[0].shape[0]
    for k, piece in enumerate(pieces):
        stack[k * w : (k + 1) * w, :] = piece[...]
    pick_rows(idx_ref, start, stack, o_ref, count)


def column_of(row, n):
    return jnp.broadcast_to(row, (128, n)).T


def half_of(parity):
    return pl.ds(pl.multiple_of(parity * HALF, HALF), HALF)


def middle_kernel(where, inv, t_own, t_sib, m_ref, mh_ref, ab_ref, d_ref, x_all, y_one):
    parity = where[0]
    x_all[:, half_of(parity)] = t_own[0:IFACE, :]
    x_all[:, half_of(1 - parity)] = t_sib[0:IFACE, :]
    y_one[...] = jnp.where(parity == 1, t_own[IFACE:EDGE, :], t_sib[IFACE:EDGE, :])

    def rows_of_m(rows):
        m_ref[rows, :] = dot(inv[rows, :], x_all[...])

    by_rows(IFACE, rows_of_m)
    mh_ref[...] = m_ref[half_of(parity), :]
    y_zero = jnp.where(parity == 0, t_own[IFACE:EDGE, :], 0.0)
    ab_ref[...] = y_zero

    def rows_of_ab(rows):
        ab_ref[rows, :] = ab_ref[rows, :] - dot_tn(t_own[0:IFACE, rows], m_ref[:, 0:HALF])

    by_rows(HALF, rows_of_ab)
    o = pl.multiple_of(parity * 128, 128)
    part = x_all[:, pl.ds(pl.multiple_of(HALF + parity * 128, 128), 128)]
    d_ref[...] = y_one[pl.ds(o, 128), :] - dot_tn(part, m_ref[:, HALF:IFACE])


def split(v):
    high = v.astype(BF16)
    return high, (v - high.astype(F32)).astype(BF16)


def three(a, b, dims=((1,), (0,))):
    def one(x, y):
        return lax.dot_general(x, y, (dims, ((), ())), preferred_element_type=F32)

    return one(a[0], b[0]) + (one(a[0], b[1]) + one(a[1], b[0]))


def side_kernel(where, inv, m, whole, gt_ref, w_ref):
    m2, inv2 = split(m[...]), split(inv[...])
    mine = half_of(where[0])

    def some(rows):
        pi = split(whole[rows, 0:IFACE])
        w_ref[rows, :] = three(pi, inv2)
        gt_ref[rows, :] = -three(pi, m2)
        gt_ref[rows, mine] = gt_ref[rows, mine] + whole[rows, IFACE:EDGE]

    by_rows(whole.shape[0], some)


def last_kernel(where, inv, m_ref, mz, mz_sib, gt, w1t, a_ref, keep2, keep_col, *refs):
    n_in = 2 * PARTS + 2 * (COLS + 1)
    ins, out = refs[:n_in], refs[n_in]
    edges, both, block, m_far, in_sems, out_sems = refs[n_in + 1 :]
    parity, quad, col = where[0], where[1], where[2]
    w = gt.shape[0]
    child = COLS * w
    copies = [[], [], [], []]

    def load(m, k, src, dst):
        c = pltpu.make_async_copy(src, dst, in_sems.at[m, k])
        c.start()
        copies[m].append(c)

    for m in range(2):
        for k in range(PARTS):
            dst = edges.at[pl.ds(m * child, child), pl.ds(k * HALF, HALF)]
            load(m, k, ins[PARTS * m + k], dst)
    for m in range(2):
        start = (2 + m) * child
        for k in range(COLS + 1):
            piece = ins[2 * PARTS + (COLS + 1) * m + k]
            load(2 + m, k, piece, edges.at[pl.ds(start, piece.shape[0]), :])
            start += piece.shape[0]

    m_far[half_of(parity), :] = mz[...]
    m_far[half_of(1 - parity), :] = mz_sib[...]
    nt = ((1,), (1,))
    inv2, near2, far2 = split(inv[...]), split(m_ref[...]), split(m_far[...])

    def some(rows):
        vt = three(split(gt[rows, :]), inv2)
        vt2 = split(vt)
        u = split((w1t[rows, :] - three(vt2, near2, nt)).T)
        f = split((-three(vt2, far2, nt)).T)
        v = split(vt.T)
        for part in range(2):
            lanes = pl.ds(pl.multiple_of(part * w + rows.start, 128), 128)
            for k in range(4):
                both[k, 0:IFACE, lanes] = (u if k < 2 else f)[part]
            for k in range(2):
                half = v[part][k * HALF : (k + 1) * HALF]
                same = k ^ parity
                both[same, IFACE:EDGE, lanes] = half
                both[same + 2, IFACE:EDGE, lanes] = half

    by_rows(w, some)

    def store(i, j):
        m, r = i * TOGETHER // COLS, i * TOGETHER % COLS + j
        o = (quad ^ m) * child + ((col + r) % COLS) * w
        return pltpu.make_async_copy(
            block.at[i % 2, pl.ds(j * w, w), :],
            out.at[pl.ds(pl.multiple_of(o, w), w), :],
            out_sems.at[i % 2, j],
        )

    def one(i, _):
        m, r = i * TOGETHER // COLS, i * TOGETHER % COLS
        for k in range(4):

            @pl.when(i == k * COLS // TOGETHER)
            def _():
                for c in copies[k]:
                    c.wait()

        @pl.when(i >= 2)
        def _():
            for j in range(TOGETHER):
                store(i - 2, j).wait()

        size = TOGETHER * w
        high, low = split(edges[pl.ds(pl.multiple_of(i * size, size), size), :])
        wide = jnp.dot(high, both[m], preferred_element_type=F32)
        total = wide[:, 0:w] + (
            wide[:, w : 2 * w] + jnp.dot(low, both[m, :, 0:w], preferred_element_type=F32)
        )
        block[i % 2] = -total

        @pl.when(m < 2)
        def _():
            own = jnp.where(m == 0, keep_col[...], 0.0)
            for j in range(TOGETHER):
                here = pl.ds(pl.multiple_of(((col + r + j) % COLS) * w, w), w)
                rows = slice(j * w, (j + 1) * w)
                mask = column_of(keep2[pl.ds(jnp.minimum(m, 1), 1), here], w)
                block[i % 2, rows] = (block[i % 2, rows] + a_ref[here, :] * own) * jnp.tile(
                    mask, (1, w // 128)
                )

        for j in range(TOGETHER):
            store(i, j).start()
        return 0

    steps = 4 * COLS // TOGETHER
    lax.fori_loop(0, steps, one, 0)
    for j in range(TOGETHER):
        store(steps - 2, j).wait()
        store(steps - 1, j).wait()


def swapped(shard, apart):
    n = lax.axis_size("box")
    return lax.ppermute(shard, "box", [(i, i ^ apart) for i in range(n)])


def shifted(shard, by):
    return lax.ppermute(shard, "col", [((i + by) % COLS, i) for i in range(COLS)])


def after(values, *others):
    return lax.optimization_barrier((values, others))[0]


def around(own, forward):
    right, left = shifted(own, 1), shifted(own, -1)
    return (own, right, left), (right if forward == 1 else left)


def farther(near, forward):
    own, right, left = near
    far = shifted(right if forward == 1 else left, forward)
    return own, right, far, left


def farther_both(near, done):
    own, right, left = near
    h = own.shape[0] // 2
    top, bottom = after((right[:h], left[h:]), done)
    far = shifted(top, 1), shifted(bottom, -1)
    return own, right, *far, left


def select(start, count, relative, pieces):
    rows = COLS * pieces[0].shape[0]
    return call(
        functools.partial(select_kernel, start, count),
        (shape(count, HALF), shape(rows, HALF)),
        1,
        COLS,
        3 * 10**9,
        8 * rows * HALF,
    )(relative, *pieces)


def merged(child_maps, iface_one, iface_two):
    a = child_maps[0]
    boundary, w = a.shape
    box, col = lax.axis_index("box"), lax.axis_index("col")
    parity = box % 2
    own_one = iface_one[0]
    group = lax.dynamic_index_in_dim(iface_two, box // 2, 0, keepdims=False)
    own_two = lax.dynamic_slice_in_dim(group, parity * HALF, HALF) - parity * boundary
    points = jnp.concatenate([own_one, own_two])

    *parts, whole = call(
        gather_kernel,
        (shape(w, HALF),) * PARTS + (shape(w, EDGE),),
        1,
        2,
        0,
        4 * boundary * w,
        [pltpu.VMEM((EDGE, w), F32)],
    )(points, a, points[None, :])
    near0, first0 = around(parts[0], 1)
    part0 = farther(near0, 1)
    relative = (points - col * w) % boundary
    where = jnp.stack([parity, box % 4, col]).astype(jnp.int32)
    near1, first1 = around(after(parts[1], first0), -1)
    part1 = farther(near1, -1)
    far = swapped(whole, 2)
    matches = jnp.arange(boundary, dtype=jnp.int32)[None, :] == points[:, None]
    keep = 1.0 - jnp.sum(matches.astype(F32), axis=0)
    keep_col = lax.dynamic_slice_in_dim(keep, col * w, w)[None, :]
    keep2 = jnp.stack([keep, swapped(keep, 1)])

    t0, stack0 = select(0, IFACE, relative, part0)
    t0, t0_sib, where, keep2, keep_col = after(
        (t0, swapped(t0, 1), where, keep2, keep_col), first1
    )
    half = call(half_one_kernel, (SQUARE,) * 3, 0, 2, HALF_COST, 10**6)(t0, t0_sib)

    right2 = shifted(after(parts[2], first0), 1)
    own2 = after(parts[2], first1)
    left2, far2 = shifted(own2, -1), shifted(own2, 2)
    part2, first2 = (parts[2], right2, far2, left2), right2
    t1, stack1 = select(HALF, HALF, relative, after(part1, half[0]))
    t1, t1_sib = after((t1, swapped(t1, 1)), first2)
    inv_one = call(
        whole_one_kernel, shape(IFACE, IFACE), 0, 5, HALF_COST, 10**6,
        [pltpu.VMEM((HALF, HALF), F32)],
    )(t1, t1_sib, *half)

    nearz, _ = around(after(far, first2), -1)
    t2, stack2 = select(0, EDGE, relative, after(part2, inv_one))
    m, m_half, ab, d = call(
        middle_kernel,
        (shape(IFACE, IFACE), shape(HALF, IFACE), SQUARE, shape(128, HALF)),
        1,
        3,
        5 * 10**9,
        2**22,
        [pltpu.VMEM((IFACE, IFACE), F32), pltpu.VMEM((HALF, HALF), F32)],
    )(where, inv_one, t2, swapped(t2, 1))

    ab_far = swapped(ab, 2)
    gt, w1t = call(
        side_kernel, (shape(w, IFACE),) * 2, 1, 3, 3 * 10**9, 2**22
    )(where, inv_one, m, whole)
    partz = farther_both(nearz, gt)
    stack0, stack1, stack2, *near = after((stack0, stack1, stack2, *partz[:2], partz[4]), gt)
    partz = near[0], near[1], partz[2], partz[3], near[2]
    ab = ab + after(ab_far, gt)
    ab_sib = swapped(ab, 1)
    d = after(d, ab_far)
    d = d + swapped(d, 2)
    d_sib = swapped(d, 1)
    half = call(half_two_kernel, (SQUARE,) * 3, 1, 2, HALF_COST, 10**6)(where, ab, ab_sib)
    stacks = (stack0, stack1, stack2)
    early = [swapped(v, 1) for v in (*stacks, partz[0], partz[1], partz[4])]
    d_mine, d_other, early = after((d, d_sib, early))
    inv_two = call(
        whole_two_kernel, shape(IFACE, IFACE), 1, 5, HALF_COST, 10**6,
        [pltpu.VMEM((HALF, HALF), F32)],
    )(where, d_mine, d_other, *half)

    m_far = swapped(after(m_half, d), 2)
    stacks_sib = early[:3]
    partz_sib = early[3], early[4], swapped(partz[2], 1), swapped(partz[3], 1), early[5]
    out = pl.pallas_call(
        last_kernel,
        name="last",
        out_shape=shape(COLS * boundary, w),
        in_specs=[SMEM] + [VMEM] * 9 + [ANY] * (2 * PARTS + 2 * (COLS + 1)),
        out_specs=ANY,
        scratch_shapes=[
            pltpu.VMEM((4 * boundary, EDGE), F32),
            pltpu.VMEM((4, EDGE, 2 * w), BF16),
            pltpu.VMEM((2, TOGETHER * w, w), F32),
            pltpu.VMEM((IFACE, IFACE), F32),
            pltpu.SemaphoreType.DMA((4, COLS + 1)),
            pltpu.SemaphoreType.DMA((2, TOGETHER)),
        ],
        cost_estimate=pl.CostEstimate(flops=10**10, bytes_accessed=3 * 10**7, transcendentals=0),
        compiler_params=pltpu.CompilerParams(vmem_limit_bytes=48 * 2**20),
    )(
        where, inv_two, m, m_far, swapped(m_far, 1), gt, w1t, a, keep2, keep_col,
        *stacks, *stacks_sib, *partz, *partz_sib,
    )
    return out[None]


def solution(mesh):
    return jax.shard_map(
        merged,
        mesh=mesh,
        in_specs=(P("box", None, "col"), P("box", None), P()),
        out_specs=P("box", None, "col"),
        check_vma=False,
    )
```
